512 devices in a mesh: mode: 64 (over y, x, core), col: 8 (over z).
Axes of the slice: x: 4, y: 8, z: 8, core: 2. Of those that a mesh axis runs over, the one named last changes fastest.
Arguments:
- tensor: float32 [512, 16, 16384], P('mode', 'col'), may hold values from -12 to 12, as said below
- initial: float32 [512, 128], replicated, may hold values from -6 to 6
Outputs:
- core_tensor: float32 [128, 16, 16384], P(None, 'col', 'mode')
- basis: float32 [512, 128], replicated
- triangle: float32 [512, 512], replicated
The draws below stay inside these ranges and needn't reach their ends.
Inputs may be any that keep to these rules, and one draw needn't show every extreme that they name: `tensor`: a float field of order one.
All inputs are finite; a program needn't handle non-finite values.
Results may differ from the reference program's by a relative error of at most 0.0003.
Values sent between devices are 32-bit elements; how exact they have to be, the bound alone decides.
A program may use at most 128 MiB of HBM per device.

```python
import math
import jax
import jax.numpy as jnp
from jax import lax

R = 512
KEEP = 128
ITERS = 3
S_DEV = 2
W_DEV = 256
S = 16
W = 16384


def draw_tensor(key, part):
    keys = jax.random.split(jax.random.fold_in(key, 17), 5)
    noise = jnp.clip(jax.random.normal(keys[0], (R, S, W), jnp.float32), -5.0, 5.0)
    row_scale = jnp.exp(jax.random.uniform(keys[1], (R,), jnp.float32, math.log(0.33), 0.0))
    block_amp = jnp.exp(jax.random.uniform(keys[2], (S // S_DEV, W // W_DEV), jnp.float32, math.log(0.1), 0.0))
    block_corr = jax.random.uniform(keys[3], (S // S_DEV, W // W_DEV), jnp.float32, 0.1, 0.45)
    amp_full = jnp.repeat(jnp.repeat(block_amp, S_DEV, 0), W_DEV, 1)
    corr_full = jnp.repeat(jnp.repeat(block_corr, S_DEV, 0), W_DEV, 1)
    rough = jax.random.uniform(keys[4], (S, W), jnp.float32, 0.5, 1.5)
    shifted = jnp.concatenate([jnp.zeros((1, S, W), jnp.float32), noise[:-1]], 0)
    mixed = noise + corr_full[None] * shifted
    return row_scale[:, None, None] * (amp_full * rough)[None] * mixed


def gaussian(rng, extent, spread, most, kind=jnp.bfloat16):
    return jnp.clip(spread * jax.random.normal(rng, extent, jnp.float32), -most, most).astype(kind)


def setup_inputs(seed: int = 0) -> dict:
    key_list = jax.random.split(jax.random.key(seed), 3)
    tensor = draw_tensor(jax.random.fold_in(key_list[2], 71), 0)
    initial = gaussian(key_list[1], (R, KEEP), 1.0, 6.0, jnp.float32)
    return dict(tensor=tensor, initial=initial)


precise = lax.Precision.HIGHEST

def reference(tensor, initial):
    column_count = S * W
    unfold = tensor.reshape(R, column_count)
    gram = jnp.dot(unfold.astype(jnp.float32), unfold.T.astype(jnp.float32), precision=precise, preferred_element_type=jnp.float32) / column_count
    triangle = jnp.linalg.cholesky(gram).T
    current = initial
    for sweep in range(ITERS):
        product = jnp.dot(gram.astype(jnp.float32), current.astype(jnp.float32), precision=precise, preferred_element_type=jnp.float32)
        inner = jnp.dot(product.T.astype(jnp.float32), product.astype(jnp.float32), precision=precise, preferred_element_type=jnp.float32)
        lower_factor = jnp.linalg.cholesky(inner)
        current = lax.linalg.triangular_solve(lower_factor, product, left_side=False, lower=True, transpose_a=True)
    core_flat = jnp.dot(current.T.astype(jnp.float32), unfold.astype(jnp.float32), precision=precise, preferred_element_type=jnp.float32)
    return (core_flat.reshape(KEEP, S, W), current, triangle)
```

```python
import functools

import jax
import jax.numpy as jnp
from jax import lax
from jax.experimental import pallas as pl
from jax.experimental.pallas import tpu as pltpu
from jax.sharding import PartitionSpec as P

MESH = pl.DeviceIdType.MESH
ITERS = 3
R = 512
NX, NY, NZ = 4, 8, 8
PLANE = 2 * NX * NY
PACK = 1280
STARTS = (0, 512, 896, 1152)
HOPS = (4, 3, 5, 2, 6, 1, 7, 0)
precise = lax.Precision.HIGHEST


def dot_nt(a, b):
    return lax.dot_general(a, b, (((1,), (1,)), ((), ())), preferred_element_type=jnp.float32)


def gather_kernel(t_ref, unf_ref, g_ref, mine, hi, lo, gp, rc, a1, rx, a2, rz, a3, ry, a4, fz, fx, fc,
                  load_sem, s_a2a, r_a2a, s_c, r_c, s_x, r_x, s_z, r_z, s_y, r_y, s_fz, r_fz, s_fx, r_fx,
                  s_fc, r_fc):
    m, z = lax.axis_index("mode"), lax.axis_index("col")
    c = lax.rem(m, 2)
    x = lax.rem(m // 2, NX)
    y = m // (2 * NX)

    def at(yy, xx, cc, zz):
        return {"mode": (yy * NX + xx) * 2 + cc, "col": zz}

    def there(k):
        dy = 4 + jnp.where(lax.rem(k // 8, 2) == 0, 1, -1) * ((k // 8 + 1) // 2)
        yy = lax.rem(y + dy, NY)
        xx = lax.rem(x + lax.rem(k // 2, NX), NX)
        cc = lax.rem(c + lax.rem(k, 2), 2)
        return (yy * NX + xx) * 2 + cc

    loads = []
    barrier = pltpu.get_barrier_semaphore()

    def load(d, carry):
        for s in range(2):
            pltpu.make_async_copy(
                t_ref.at[:, s, pl.ds(pl.multiple_of(d * 256, 256), 256)],
                mine.at[d, :, pl.ds(s * 256, 256)],
                load_sem.at[s, d],
            ).start()
        return carry

    lax.fori_loop(0, PLANE, load, 0)

    def greet(k, carry):
        pl.semaphore_signal(barrier, inc=1, device_id={"mode": lax.rem(m + k, PLANE), "col": z}, device_id_type=MESH)
        return carry

    lax.fori_loop(1, PLANE, greet, 0)

    def greet_z(k, carry):
        pl.semaphore_signal(barrier, inc=1, device_id={"mode": m, "col": lax.rem(z + k, NZ)}, device_id_type=MESH)
        return carry

    lax.fori_loop(1, NZ, greet_z, 0)
    pl.semaphore_wait(barrier, PLANE - 1 + NZ - 1)

    def loaded(d, carry):
        for s in range(2):
            pltpu.make_async_copy(
                t_ref.at[:, s, pl.ds(pl.multiple_of(d * 256, 256), 256)],
                mine.at[d, :, pl.ds(s * 256, 256)],
                load_sem.at[s, d],
            ).wait()
        return carry

    lax.fori_loop(0, PLANE, loaded, 0)

    def plane_copy(d, src):
        return pltpu.make_async_remote_copy(
            mine.at[d], unf_ref.at[src], s_a2a.at[d], r_a2a.at[src],
            device_id={"mode": d, "col": z}, device_id_type=MESH)

    def send(k, carry):
        d = lax.rem(m + k, PLANE)
        plane_copy(d, m).start()
        return carry

    lax.fori_loop(1, PLANE, send, 0)
    own = pltpu.make_async_copy(mine.at[m], unf_ref.at[m], load_sem.at[0, 0])
    own.start()
    own.wait()

    def arrived(k, carry):
        d = lax.rem(m + k, PLANE)
        plane_copy(d, d).wait()
        return carry

    lax.fori_loop(1, PLANE, arrived, 0)

    unfold = unf_ref[...].reshape(R, 512)
    high = unfold.astype(jnp.bfloat16)
    hi[...] = high
    lo[...] = (unfold - high.astype(jnp.float32)).astype(jnp.bfloat16)
    scale = 1.0 / (512 * PLANE * NZ)
    for i in range(4):
        h = hi[pl.ds(i * 128, 128), :]
        l = lo[pl.ds(i * 128, 128), :]
        rest = pl.ds(i * 128, R - i * 128)
        part = dot_nt(h, hi[rest, :]) + (dot_nt(h, lo[rest, :]) + dot_nt(l, hi[rest, :]))
        gp[:, :, pl.ds(STARTS[i], R - i * 128)] = (part * scale).reshape(16, 8, R - i * 128)

    half = pltpu.make_async_remote_copy(
        gp.at[pl.ds((1 - c) * 8, 8)], rc, s_c, r_c, device_id=at(y, x, 1 - c, z), device_id_type=MESH)
    half.start()
    half.wait()
    a1[...] = gp[pl.ds(c * 8, 8)] + rc[...]

    def x_copy(to, src):
        return pltpu.make_async_remote_copy(
            a1.at[pl.ds(2 * to, 2)], rx.at[src], s_x.at[to], r_x.at[src],
            device_id=at(y, to, c, z), device_id_type=MESH)

    for k in (2, 1, 3):
        x_copy(lax.rem(x + k, NX), x).start()
    rx[x] = a1[pl.ds(2 * x, 2)]
    for k in (1, 3, 2):
        to = lax.rem(x + k, NX)
        x_copy(to, to).wait()
    total = (rx[0] + rx[1]) + (rx[2] + rx[3])
    for rg in range(2):
        for q in range(3):
            a2[rg * 4 + q] = total[rg, :, q * 384:(q + 1) * 384]
        a2[rg * 4 + 3] = jnp.concatenate([total[rg, :, 1152:], jnp.zeros((8, 256), jnp.float32)], axis=1)

    def z_copy(to, src):
        return pltpu.make_async_remote_copy(
            a2.at[to], rz.at[src], s_z.at[to], r_z.at[src], device_id=at(y, x, c, to), device_id_type=MESH)

    for k in (4, 3, 5, 2, 6, 1, 7):
        z_copy(lax.rem(z + k, NZ), z).start()
    rz[z] = a2[z]
    for k in (1, 7, 2, 6, 3, 5, 4):
        to = lax.rem(z + k, NZ)
        z_copy(to, to).wait()
    a3[...] = ((rz[0] + rz[1]) + (rz[2] + rz[3])) + ((rz[4] + rz[5]) + (rz[6] + rz[7]))

    def y_copy(to, src):
        return pltpu.make_async_remote_copy(
            a3, ry.at[src], s_y.at[to], r_y.at[src], device_id=at(to, x, c, z), device_id_type=MESH)

    for k in (4, 3, 5, 2, 6, 1, 7):
        y_copy(lax.rem(y + k, NY), y).start()
    ry[y] = a3[...]
    for k in (1, 7, 2, 6, 3, 5, 4):
        to = lax.rem(y + k, NY)
        y_copy(to, to).wait()
    a4[...] = ((ry[0] + ry[1]) + (ry[2] + ry[3])) + ((ry[4] + ry[5]) + (ry[6] + ry[7]))

    def fz_copy(to, src):
        return pltpu.make_async_remote_copy(
            a4, fz.at[src], s_fz.at[to], r_fz.at[src], device_id=at(y, x, c, to), device_id_type=MESH)

    for k in (4, 3, 5, 2, 6, 1, 7):
        fz_copy(lax.rem(z + k, NZ), z).start()
    fz[z] = a4[...]
    for k in (1, 7, 2, 6, 3, 5, 4):
        to = lax.rem(z + k, NZ)
        fz_copy(to, to).wait()

    def fx_copy(to, src):
        return pltpu.make_async_remote_copy(
            fz, fx.at[src], s_fx.at[to], r_fx.at[src], device_id=at(y, to, c, z), device_id_type=MESH)

    for k in (2, 1, 3):
        fx_copy(lax.rem(x + k, NX), x).start()
    fx[x] = fz[...]
    for k in (1, 3, 2):
        to = lax.rem(x + k, NX)
        fx_copy(to, to).wait()
    other = pltpu.make_async_remote_copy(
        fx, fc.at[c], s_fc, r_fc, device_id=at(y, x, 1 - c, z), device_id_type=MESH)
    other.start()
    fc[c] = fx[...]
    pltpu.make_async_remote_copy(
        fx, fc.at[1 - c], s_fc, r_fc, device_id=at(y, x, 1 - c, z), device_id_type=MESH).wait()

    whole = fc[...].reshape(16, 4, 8, 384)
    packed = jnp.concatenate([whole[:, q] for q in range(4)], axis=2)
    for i in range(4):
        wide = packed[:, :, STARTS[i]:STARTS[i] + R - i * 128].reshape(128, R - i * 128)
        g_ref[pl.ds(i * 128, 128), pl.ds(i * 128, R - i * 128)] = wide
        for j in range(i + 1, 4):
            g_ref[pl.ds(j * 128, 128), pl.ds(i * 128, 128)] = wide[:, (j - i) * 128:(j - i + 1) * 128].T


def gathered(tensor):
    f32 = jnp.float32
    dma = pltpu.SemaphoreType.DMA
    vmem = pl.BlockSpec(memory_space=pltpu.VMEM)
    return pl.pallas_call(
        gather_kernel,
        out_shape=(jax.ShapeDtypeStruct((PLANE, 8, 512), f32), jax.ShapeDtypeStruct((R, R), f32)),
        in_specs=[pl.BlockSpec(memory_space=pl.ANY)],
        out_specs=(vmem, vmem),
        scratch_shapes=[
            pltpu.VMEM((PLANE, 8, 512), f32),
            pltpu.VMEM((R, 512), jnp.bfloat16),
            pltpu.VMEM((R, 512), jnp.bfloat16),
            pltpu.VMEM((16, 8, PACK), f32),
            pltpu.VMEM((8, 8, PACK), f32),
            pltpu.VMEM((8, 8, PACK), f32),
            pltpu.VMEM((NX, 2, 8, PACK), f32),
            pltpu.VMEM((8, 8, 384), f32),
            pltpu.VMEM((NZ, 8, 384), f32),
            pltpu.VMEM((8, 384), f32),
            pltpu.VMEM((NY, 8, 384), f32),
            pltpu.VMEM((8, 384), f32),
            pltpu.VMEM((NZ, 8, 384), f32),
            pltpu.VMEM((NX, NZ, 8, 384), f32),
            pltpu.VMEM((2, NX, NZ, 8, 384), f32),
            dma((2, PLANE)), dma((PLANE,)), dma((PLANE,)), dma, dma, dma((NX,)), dma((NX,)),
            dma((NZ,)), dma((NZ,)), dma((NY,)), dma((NY,)), dma((NZ,)), dma((NZ,)), dma((NX,)), dma((NX,)),
            dma, dma,
        ],
        compiler_params=pltpu.CompilerParams(
            collective_id=0, has_side_effects=True, vmem_limit_bytes=40 * 2**20),
    )(tensor)


def local(tensor, initial):
    blocks, gram_sum = gathered(tensor)
    unfold = blocks.reshape(R, 512)
    triangle = jnp.linalg.cholesky(gram_sum).T
    current = initial
    for sweep in range(ITERS):
        product = jnp.dot(gram_sum, current, precision=precise, preferred_element_type=jnp.float32)
        inner = jnp.dot(product.T, product, precision=precise, preferred_element_type=jnp.float32)
        lower_factor = jnp.linalg.cholesky(inner)
        current = lax.linalg.triangular_solve(
            lower_factor, product, left_side=False, lower=True, transpose_a=True)
    core_flat = jnp.dot(current.T, unfold, precision=precise, preferred_element_type=jnp.float32)
    return core_flat.reshape(current.shape[1], 2, 256), current, triangle


def solution(mesh):
    return jax.shard_map(
        local,
        mesh=mesh,
        in_specs=(P("mode", "col", None), P()),
        out_specs=(P(None, "col", "mode"), P(), P()),
        check_vma=False,
    )
```

```python
import functools

import jax
import jax.numpy as jnp
from jax import lax
from jax.experimental import pallas as pl
from jax.experimental.pallas import tpu as pltpu
from jax.sharding import PartitionSpec as P

MESH = pl.DeviceIdType.MESH
ITERS = 3
R = 512
NX, NY, NZ = 4, 8, 8
PLANE = 2 * NX * NY
PACK = 1280
STARTS = (0, 512, 896, 1152)
N = 128
precise = lax.Precision.HIGHEST


def dot_nt(a, b):
    return lax.dot_general(a, b, (((1,), (1,)), ((), ())), preferred_element_type=jnp.float32)


def gather_kernel(t_ref, unf_ref, g_ref, mine, hi, lo, gp, rc, a1, rx, a2, rz, a3, ry, a4, fz, fx, fc,
                  load_sem, s_a2a, r_a2a, s_c, r_c, s_x, r_x, s_z, r_z, s_y, r_y, s_fz, r_fz, s_fx, r_fx,
                  s_fc, r_fc):
    m, z = lax.axis_index("mode"), lax.axis_index("col")
    c = lax.rem(m, 2)
    x = lax.rem(m // 2, NX)
    y = m // (2 * NX)

    def at(yy, xx, cc, zz):
        return {"mode": (yy * NX + xx) * 2 + cc, "col": zz}

    barrier = pltpu.get_barrier_semaphore()

    def load(d, carry):
        for s in range(2):
            pltpu.make_async_copy(
                t_ref.at[:, s, pl.ds(pl.multiple_of(d * 256, 256), 256)],
                mine.at[d, :, pl.ds(s * 256, 256)],
                load_sem.at[s, d],
            ).start()
        return carry

    lax.fori_loop(0, PLANE, load, 0)

    def greet(k, carry):
        pl.semaphore_signal(barrier, inc=1, device_id={"mode": lax.rem(m + k, PLANE), "col": z}, device_id_type=MESH)
        return carry

    lax.fori_loop(1, PLANE, greet, 0)

    def greet_z(k, carry):
        pl.semaphore_signal(barrier, inc=1, device_id={"mode": m, "col": lax.rem(z + k, NZ)}, device_id_type=MESH)
        return carry

    lax.fori_loop(1, NZ, greet_z, 0)
    pl.semaphore_wait(barrier, PLANE - 1 + NZ - 1)

    def loaded(d, carry):
        for s in range(2):
            pltpu.make_async_copy(
                t_ref.at[:, s, pl.ds(pl.multiple_of(d * 256, 256), 256)],
                mine.at[d, :, pl.ds(s * 256, 256)],
                load_sem.at[s, d],
            ).wait()
        return carry

    lax.fori_loop(0, PLANE, loaded, 0)

    def plane_copy(d, src):
        return pltpu.make_async_remote_copy(
            mine.at[d], unf_ref.at[src], s_a2a.at[d], r_a2a.at[src],
            device_id={"mode": d, "col": z}, device_id_type=MESH)

    def send(k, carry):
        d = lax.rem(m + k, PLANE)
        plane_copy(d, m).start()
        return carry

    lax.fori_loop(1, PLANE, send, 0)
    own = pltpu.make_async_copy(mine.at[m], unf_ref.at[m], load_sem.at[0, 0])
    own.start()
    own.wait()

    def arrived(k, carry):
        d = lax.rem(m + k, PLANE)
        plane_copy(d, d).wait()
        return carry

    lax.fori_loop(1, PLANE, arrived, 0)

    unfold = unf_ref[...].reshape(R, 512)
    high = unfold.astype(jnp.bfloat16)
    hi[...] = high
    lo[...] = (unfold - high.astype(jnp.float32)).astype(jnp.bfloat16)
    scale = 1.0 / (512 * PLANE * NZ)
    for i in range(4):
        h = hi[pl.ds(i * 128, 128), :]
        l = lo[pl.ds(i * 128, 128), :]
        rest = pl.ds(i * 128, R - i * 128)
        part = dot_nt(h, hi[rest, :]) + (dot_nt(h, lo[rest, :]) + dot_nt(l, hi[rest, :]))
        gp[:, :, pl.ds(STARTS[i], R - i * 128)] = (part * scale).reshape(16, 8, R - i * 128)

    half = pltpu.make_async_remote_copy(
        gp.at[pl.ds((1 - c) * 8, 8)], rc, s_c, r_c, device_id=at(y, x, 1 - c, z), device_id_type=MESH)
    half.start()
    half.wait()
    a1[...] = gp[pl.ds(c * 8, 8)] + rc[...]

    def x_copy(to, src):
        return pltpu.make_async_remote_copy(
            a1.at[pl.ds(2 * to, 2)], rx.at[src], s_x.at[to], r_x.at[src],
            device_id=at(y, to, c, z), device_id_type=MESH)

    for k in (2, 1, 3):
        x_copy(lax.rem(x + k, NX), x).start()
    rx[x] = a1[pl.ds(2 * x, 2)]
    for k in (1, 3, 2):
        to = lax.rem(x + k, NX)
        x_copy(to, to).wait()
    total = (rx[0] + rx[1]) + (rx[2] + rx[3])
    for rg in range(2):
        for q in range(3):
            a2[rg * 4 + q] = total[rg, :, q * 384:(q + 1) * 384]
        a2[rg * 4 + 3] = jnp.concatenate([total[rg, :, 1152:], jnp.zeros((8, 256), jnp.float32)], axis=1)

    def z_copy(to, src):
        return pltpu.make_async_remote_copy(
            a2.at[to], rz.at[src], s_z.at[to], r_z.at[src], device_id=at(y, x, c, to), device_id_type=MESH)

    for k in (4, 3, 5, 2, 6, 1, 7):
        z_copy(lax.rem(z + k, NZ), z).start()
    rz[z] = a2[z]
    for k in (1, 7, 2, 6, 3, 5, 4):
        to = lax.rem(z + k, NZ)
        z_copy(to, to).wait()
    a3[...] = ((rz[0] + rz[1]) + (rz[2] + rz[3])) + ((rz[4] + rz[5]) + (rz[6] + rz[7]))

    def y_copy(to, src):
        return pltpu.make_async_remote_copy(
            a3, ry.at[src], s_y.at[to], r_y.at[src], device_id=at(to, x, c, z), device_id_type=MESH)

    for k in (4, 3, 5, 2, 6, 1, 7):
        y_copy(lax.rem(y + k, NY), y).start()
    ry[y] = a3[...]
    for k in (1, 7, 2, 6, 3, 5, 4):
        to = lax.rem(y + k, NY)
        y_copy(to, to).wait()
    a4[...] = ((ry[0] + ry[1]) + (ry[2] + ry[3])) + ((ry[4] + ry[5]) + (ry[6] + ry[7]))

    def fz_copy(to, src):
        return pltpu.make_async_remote_copy(
            a4, fz.at[src], s_fz.at[to], r_fz.at[src], device_id=at(y, x, c, to), device_id_type=MESH)

    for k in (4, 3, 5, 2, 6, 1, 7):
        fz_copy(lax.rem(z + k, NZ), z).start()
    fz[z] = a4[...]
    for k in (1, 7, 2, 6, 3, 5, 4):
        to = lax.rem(z + k, NZ)
        fz_copy(to, to).wait()

    def fx_copy(to, src):
        return pltpu.make_async_remote_copy(
            fz, fx.at[src], s_fx.at[to], r_fx.at[src], device_id=at(y, to, c, z), device_id_type=MESH)

    for k in (2, 1, 3):
        fx_copy(lax.rem(x + k, NX), x).start()
    fx[x] = fz[...]
    for k in (1, 3, 2):
        to = lax.rem(x + k, NX)
        fx_copy(to, to).wait()
    other = pltpu.make_async_remote_copy(
        fx, fc.at[c], s_fc, r_fc, device_id=at(y, x, 1 - c, z), device_id_type=MESH)
    other.start()
    fc[c] = fx[...]
    pltpu.make_async_remote_copy(
        fx, fc.at[1 - c], s_fc, r_fc, device_id=at(y, x, 1 - c, z), device_id_type=MESH).wait()

    whole = fc[...].reshape(16, 4, 8, 384)
    packed = jnp.concatenate([whole[:, q] for q in range(4)], axis=2)
    for i in range(4):
        wide = packed[:, :, STARTS[i]:STARTS[i] + R - i * 128].reshape(128, R - i * 128)
        g_ref[pl.ds(i * 128, 128), pl.ds(i * 128, R - i * 128)] = wide
        for j in range(i + 1, 4):
            g_ref[pl.ds(j * 128, 128), pl.ds(i * 128, 128)] = wide[:, (j - i) * 128:(j - i + 1) * 128].T


def gathered(tensor):
    f32 = jnp.float32
    dma = pltpu.SemaphoreType.DMA
    vmem = pl.BlockSpec(memory_space=pltpu.VMEM)
    return pl.pallas_call(
        gather_kernel,
        out_shape=(jax.ShapeDtypeStruct((PLANE, 8, 512), f32), jax.ShapeDtypeStruct((R, R), f32)),
        in_specs=[pl.BlockSpec(memory_space=pl.ANY)],
        out_specs=(vmem, vmem),
        scratch_shapes=[
            pltpu.VMEM((PLANE, 8, 512), f32),
            pltpu.VMEM((R, 512), jnp.bfloat16),
            pltpu.VMEM((R, 512), jnp.bfloat16),
            pltpu.VMEM((16, 8, PACK), f32),
            pltpu.VMEM((8, 8, PACK), f32),
            pltpu.VMEM((8, 8, PACK), f32),
            pltpu.VMEM((NX, 2, 8, PACK), f32),
            pltpu.VMEM((8, 8, 384), f32),
            pltpu.VMEM((NZ, 8, 384), f32),
            pltpu.VMEM((8, 384), f32),
            pltpu.VMEM((NY, 8, 384), f32),
            pltpu.VMEM((8, 384), f32),
            pltpu.VMEM((NZ, 8, 384), f32),
            pltpu.VMEM((NX, NZ, 8, 384), f32),
            pltpu.VMEM((2, NX, NZ, 8, 384), f32),
            dma((2, PLANE)), dma((PLANE,)), dma((PLANE,)), dma, dma, dma((NX,)), dma((NX,)),
            dma((NZ,)), dma((NZ,)), dma((NY,)), dma((NY,)), dma((NZ,)), dma((NZ,)), dma((NX,)), dma((NX,)),
            dma, dma,
        ],
        compiler_params=pltpu.CompilerParams(
            collective_id=0, has_side_effects=True, vmem_limit_bytes=40 * 2**20),
    )(tensor)


def dot_full(a, b, da, db):
    return lax.dot_general(
        a, b, (((da,), (db,)), ((), ())), precision=precise, preferred_element_type=jnp.float32)


def row_of(tile, j):
    return jnp.broadcast_to(tile[j:j + 1, :], (8, N))


def column_of(tile, j):
    return jnp.broadcast_to(tile[:, j:j + 1], (8, N))


def factor(a_ref, w_ref, u_ref, v_ref):
    rows, columns = (lax.broadcasted_iota(jnp.int32, (N, N), d) for d in range(2))
    w_ref[...] = (rows == columns).astype(jnp.float32)
    line = lax.broadcasted_iota(jnp.int32, (8, N), 0)

    def eliminate(step, carry):
        a = [a_ref[8 * i:8 * i + 8, :] for i in range(4)]
        w = [w_ref[8 * i:8 * i + 8, :] for i in range(4)]
        for p in range(4):
            lanes = {i: [column_of(a[i], 8 * p + c) for c in range(8)] for i in range(p, 4)}
            pivots = jnp.zeros((8, N), jnp.float32)
            for j in range(8):
                pivot = row_of(lanes[p][j], j)
                inverse = 1.0 / pivot
                pivots = jnp.where(line == j, pivot, pivots)
                row_a, row_w = row_of(a[p], j), row_of(w[p], j)
                row_lanes = {c: row_of(lanes[p][c], j) for c in range(j + 1, 8)}
                for i in range(p, 4):
                    ratio = lanes[i][j] * inverse
                    if i == p:
                        ratio = jnp.where(line > j, ratio, 0.0)
                    a[i] = a[i] - ratio * row_a
                    w[i] = w[i] - ratio * row_w
                    for c in range(j + 1, 8):
                        lanes[i][c] = lanes[i][c] - ratio * row_lanes[c]
            root = lax.rsqrt(pivots)
            root = root * (1.5 - 0.5 * (pivots * root) * root)
            a[p] = a[p] * root
            w[p] = w[p] * root
        upper = jnp.concatenate(a, axis=0)
        lower_inverse = jnp.concatenate(w, axis=0)
        here = pl.ds(pl.multiple_of(step * 32, 32), 32)
        u_ref[here, :] = pltpu.roll(upper, step * 32, 1)
        v_ref[here, :] = lower_inverse
        update = dot_full(upper, jnp.concatenate([upper, lower_inverse], axis=1), 0, 0)
        a_ref[0:96, :] = pltpu.roll(a_ref[32:N, :] - update[32:N, :N], 96, 1)
        w_ref[0:96, :] = w_ref[32:N, :] - update[32:N, N:]
        return carry

    lax.fori_loop(0, N // 32, eliminate, 0)
    u_ref[...] = jnp.where(rows <= columns, u_ref[...], 0.0)


def factor_kernel(g_ref, initial_ref, basis_ref, triangle_ref, rest_ref, product_ref, a_ref, w_ref, u_ref, v_ref):
    c = lax.rem(lax.axis_index("mode"), 2)

    @pl.when(c == 0)
    def _():
        rest_ref[...] = g_ref[...]
        triangle_ref[...] = jnp.zeros((R, R), jnp.float32)
        for k in range(4):
            own, after = pl.ds(k * N, N), pl.ds((k + 1) * N, R - (k + 1) * N)
            a_ref[...] = rest_ref[own, own]
            factor(a_ref, w_ref, u_ref, v_ref)
            triangle_ref[own, own] = u_ref[...]
            if k < 3:
                panel = dot_full(v_ref[...], rest_ref[own, after], 1, 0)
                triangle_ref[own, after] = panel
                for i in range(k + 1, 4):
                    left = panel[:, (i - k - 1) * N:(i - k) * N]
                    right = panel[:, (i - k - 1) * N:]
                    rest_ref[pl.ds(i * N, N), pl.ds(i * N, R - i * N)] -= dot_full(left, right, 0, 0)

    @pl.when(c == 1)
    def _():
        basis_ref[...] = initial_ref[...]

        def sweep(step, carry):
            product = dot_full(g_ref[...], basis_ref[...], 1, 0)
            product_ref[...] = product
            a_ref[...] = dot_full(product, product, 0, 0)
            factor(a_ref, w_ref, u_ref, v_ref)
            basis_ref[...] = dot_full(product_ref[...], v_ref[...], 1, 1)
            return carry

        lax.fori_loop(0, ITERS, sweep, 0)


def factored(gram, initial):
    f32 = jnp.float32
    vmem = pl.BlockSpec(memory_space=pltpu.VMEM)
    square = pltpu.VMEM((N, N), f32)
    return pl.pallas_call(
        factor_kernel,
        out_shape=(jax.ShapeDtypeStruct((R, N), f32), jax.ShapeDtypeStruct((R, R), f32)),
        in_specs=[vmem, vmem],
        out_specs=(vmem, vmem),
        scratch_shapes=[pltpu.VMEM((R, R), f32), pltpu.VMEM((R, N), f32), square, square, square, square],
        compiler_params=pltpu.CompilerParams(vmem_limit_bytes=16 * 2**20),
    )(gram, initial)


def exchange_kernel(basis_ref, triangle_ref, basis_out, triangle_out, send_sem, recv_sem, own_sem):
    m, z = lax.axis_index("mode"), lax.axis_index("col")
    c = lax.rem(m, 2)
    partner = {"mode": m + 1 - 2 * c, "col": z}
    barrier = pltpu.get_barrier_semaphore()
    pl.semaphore_signal(barrier, inc=1, device_id=partner, device_id_type=MESH)
    pl.semaphore_wait(barrier, 1)

    def over(src, dst):
        return pltpu.make_async_remote_copy(
            src, dst, send_sem, recv_sem, device_id=partner, device_id_type=MESH)

    @pl.when(c == 0)
    def _():
        over(triangle_ref, triangle_out).start()
        own = pltpu.make_async_copy(triangle_ref, triangle_out, own_sem)
        own.start()
        own.wait()
        over(basis_ref, basis_out).wait_recv()
        over(triangle_ref, triangle_out).wait_send()

    @pl.when(c == 1)
    def _():
        over(basis_ref, basis_out).start()
        own = pltpu.make_async_copy(basis_ref, basis_out, own_sem)
        own.start()
        own.wait()
        over(triangle_ref, triangle_out).wait_recv()
        over(basis_ref, basis_out).wait_send()


def exchanged(basis, triangle):
    dma = pltpu.SemaphoreType.DMA
    vmem = pl.BlockSpec(memory_space=pltpu.VMEM)
    return pl.pallas_call(
        exchange_kernel,
        out_shape=tuple(jax.ShapeDtypeStruct(a.shape, a.dtype) for a in (basis, triangle)),
        in_specs=[vmem, vmem],
        out_specs=(vmem, vmem),
        scratch_shapes=[dma, dma, dma],
        compiler_params=pltpu.CompilerParams(
            collective_id=1, has_side_effects=True, vmem_limit_bytes=8 * 2**20),
    )(basis, triangle)


def core_kernel(basis_ref, blocks_ref, core_ref):
    unfold = blocks_ref[...].reshape(R, 512)
    core = dot_full(basis_ref[...], unfold, 0, 0)
    for s in range(2):
        core_ref[:, s, :] = core[:, s * 256:(s + 1) * 256]


def projected(basis, blocks):
    vmem = pl.BlockSpec(memory_space=pltpu.VMEM)
    return pl.pallas_call(
        core_kernel,
        out_shape=jax.ShapeDtypeStruct((N, 2, 256), jnp.float32),
        in_specs=[vmem, vmem],
        out_specs=vmem,
        compiler_params=pltpu.CompilerParams(vmem_limit_bytes=16 * 2**20),
    )(basis, blocks)


def local(tensor, initial):
    blocks, gram = gathered(tensor)
    basis, triangle = exchanged(*factored(gram, initial))
    return projected(basis, blocks), basis, triangle


def solution(mesh):
    return jax.shard_map(
        local,
        mesh=mesh,
        in_specs=(P("mode", "col", None), P()),
        out_specs=(P(None, "col", "mode"), P(), P()),
        check_vma=False,
    )
```

```python
import functools

import jax
import jax.numpy as jnp
from jax import lax
from jax.experimental import pallas as pl
from jax.experimental.pallas import tpu as pltpu
from jax.sharding import PartitionSpec as P

MESH = pl.DeviceIdType.MESH
ITERS = 3
R = 512
NX, NY, NZ = 4, 8, 8
PLANE = 2 * NX * NY
STARTS = (0, 512, 896, 1152)
N = 128
VM = 40
precise = lax.Precision.HIGHEST


def dot_nt(a, b):
    return lax.dot_general(a, b, (((1,), (1,)), ((), ())), preferred_element_type=jnp.float32)


def gather_kernel(t_ref, unf_ref, g_ref, hi, lo, gp, rc, rx, a2, rz, a3, ry, full,
                  own_sem, s_a2a, r_a2a, s_c, r_c, s_x, r_x, s_z, r_z, s_y, r_y,
                  s_fz, s_fx, s_fc, r_full):
    m, z = lax.axis_index("mode"), lax.axis_index("col")
    c = lax.rem(m, 2)
    x = lax.rem(m // 2, NX)
    y = m // (2 * NX)

    def index(yy, xx, cc):
        return (yy * NX + xx) * 2 + cc

    def remote(src, dst, send_sem, recv_sem, mode, col):
        return pltpu.make_async_remote_copy(
            src, dst, send_sem, recv_sem, device_id={"mode": mode, "col": col}, device_id_type=MESH)

    barrier = pltpu.get_barrier_semaphore()

    def greet(k, carry):
        pl.semaphore_signal(barrier, inc=1, device_id={"mode": lax.rem(m + k, PLANE), "col": z}, device_id_type=MESH)
        return carry

    def greet_z(k, carry):
        pl.semaphore_signal(barrier, inc=1, device_id={"mode": m, "col": lax.rem(z + k, NZ)}, device_id_type=MESH)
        return carry

    lax.fori_loop(1, PLANE, greet, 0)
    lax.fori_loop(1, NZ, greet_z, 0)
    pl.semaphore_wait(barrier, PLANE - 1 + NZ - 1)

    def near(dy, dx, dc):
        return index(lax.rem(y + dy, NY), lax.rem(x + dx, NX), lax.rem(c + dc, 2))

    def columns(d, s):
        return t_ref.at[:, s, pl.ds(pl.multiple_of(d * 256, 256), 256)]

    def slab(src, s):
        return unf_ref.at[src, :, pl.ds(s * 256, 256)]

    def straight(d, src, s):
        return remote(columns(d, s), slab(src, s), s_a2a.at[s, d], r_a2a.at[s, src], d, z)

    def send(k, carry):
        for dy in (4, 1, 7, 2, 6, 3, 5, 0):
            for s in range(2):
                straight(near(dy, k // 2, lax.rem(k, 2)), m, s).start()
        return carry

    for dy in (4, 1, 7, 2, 6, 3, 5):
        for s in range(2):
            straight(near(dy, 0, 0), m, s).start()
    lax.fori_loop(1, 2 * NX, send, 0)
    own = [pltpu.make_async_copy(columns(m, s), slab(m, s), own_sem.at[s]) for s in range(2)]
    for copy in own:
        copy.start()
    for copy in own:
        copy.wait()

    def arrived(k, carry):
        d = lax.rem(m + k, PLANE)
        for s in range(2):
            straight(d, d, s).wait()
        return carry

    lax.fori_loop(1, PLANE, arrived, 0)

    unfold = unf_ref[...].reshape(R, 512)
    high = unfold.astype(jnp.bfloat16)
    hi[...] = high
    lo[...] = (unfold - high.astype(jnp.float32)).astype(jnp.bfloat16)
    scale = 1.0 / (512 * PLANE * NZ)
    gp[...] = jnp.zeros_like(gp)
    for i in range(4):
        h = hi[pl.ds(i * N, N), :]
        l = lo[pl.ds(i * N, N), :]
        rest = pl.ds(i * N, R - i * N)
        part = (dot_nt(h, hi[rest, :]) + (dot_nt(h, lo[rest, :]) + dot_nt(l, hi[rest, :]))) * scale
        for j in range(4 - i):
            tile = part[:, j * N:(j + 1) * N].reshape(8, 2, 8, N)
            q, lane = divmod(STARTS[i] // N + j, 3)
            for rg in range(2):
                gp[:, rg * 4 + q, :, lane * N:(lane + 1) * N] = tile[:, rg]

    def c_copy(to):
        return remote(gp.at[(1 - c) * NX + to], rc.at[to], s_c.at[to], r_c.at[to], index(y, x, 1 - c), z)

    ring_x = [lax.rem(x + k, NX) for k in (2, 1, 3, 0)]
    ring_z = [lax.rem(z + k, NZ) for k in (4, 3, 5, 2, 6, 1, 7)]
    for to in ring_x:
        c_copy(to).start()
    for to in ring_x:
        c_copy(to).wait()
        rc[to] += gp[c * NX + to]

    def x_copy(to, piece, src):
        return remote(rc.at[to, piece], rx.at[src, piece], s_x.at[to, piece], r_x.at[src, piece], index(y, to, c), z)

    def z_copy(to, src):
        return remote(a2.at[to], rz.at[src], s_z.at[to], r_z.at[src], m, to)

    for piece in ring_z + [z]:
        for to in ring_x[:3]:
            x_copy(to, piece, x).start()
    rx[x] = rc[x]
    for piece in ring_z + [z]:
        for to in ring_x[:3]:
            x_copy(to, piece, to).wait_recv()
        a2[piece] = (rx[0, piece] + rx[1, piece]) + (rx[2, piece] + rx[3, piece])
        if piece is not z:
            z_copy(piece, z).start()
    rz[z] = a2[z]
    for to in reversed(ring_z):
        z_copy(to, to).wait()
    a3[...] = ((rz[0] + rz[1]) + (rz[2] + rz[3])) + ((rz[4] + rz[5]) + (rz[6] + rz[7]))

    def y_copy(to, src):
        return remote(a3, ry.at[src], s_y.at[to], r_y.at[src], index(to, x, c), z)

    ring_y = [lax.rem(y + k, NY) for k in (4, 3, 5, 2, 6, 1, 7)]
    for to in ring_y:
        y_copy(to, y).start()
    ry[y] = a3[...]
    for to in reversed(ring_y):
        y_copy(to, to).wait()
    full[c, x, z] = ((ry[0] + ry[1]) + (ry[2] + ry[3])) + ((ry[4] + ry[5]) + (ry[6] + ry[7]))

    def fz_copy(to, src):
        return remote(full.at[c, x, src], full.at[c, x, src], s_fz.at[to], r_full.at[c, x, src], m, to)

    def fx_copy(to, src, piece):
        return remote(full.at[c, src, piece], full.at[c, src, piece], s_fx.at[to, piece], r_full.at[c, src, piece], index(y, to, c), z)

    def fc_copy(cc, xx, piece):
        return remote(full.at[cc, xx, piece], full.at[cc, xx, piece], s_fc.at[xx, piece], r_full.at[cc, xx, piece], index(y, x, 1 - c), z)

    def pass_on(piece):
        for to in ring_x[:3]:
            fx_copy(to, x, piece).start()
        fc_copy(c, x, piece).start()

    for to in ring_z:
        fz_copy(to, z).start()
    pass_on(z)
    for src in reversed(ring_z):
        fz_copy(src, src).wait_recv()
        pass_on(src)
    for piece in [z] + ring_z[::-1]:
        for src in (ring_x[1], ring_x[2], ring_x[0]):
            fx_copy(src, src, piece).wait_recv()
            fc_copy(c, src, piece).start()

    def from_core(k, carry):
        fc_copy(1 - c, k // NZ, lax.rem(k, NZ)).wait_recv()
        return carry

    lax.fori_loop(0, NX * NZ, from_core, 0)

    whole = full[...].reshape(16, 4, 8, 384)
    for i in range(4):
        for j in range(i, 4):
            q, lane = divmod(STARTS[i] // N + j - i, 3)
            block = whole[:, q, :, lane * N:(lane + 1) * N].reshape(N, N)
            g_ref[pl.ds(i * N, N), pl.ds(j * N, N)] = block
            if i != j:
                g_ref[pl.ds(j * N, N), pl.ds(i * N, N)] = block.T

    def sent_x(k, carry):
        for to in ring_x[:3]:
            x_copy(to, k, x).wait_send()
            fx_copy(to, x, k).wait_send()
        return carry

    def sent_c(k, carry):
        fc_copy(c, k // NZ, lax.rem(k, NZ)).wait_send()
        return carry

    lax.fori_loop(0, NZ, sent_x, 0)
    lax.fori_loop(0, NX * NZ, sent_c, 0)
    for to in ring_z:
        fz_copy(to, z).wait_send()


def gathered(tensor):
    f32 = jnp.float32
    dma = pltpu.SemaphoreType.DMA
    vmem = pl.BlockSpec(memory_space=pltpu.VMEM)
    piece = (8, 384)
    return pl.pallas_call(
        gather_kernel,
        out_shape=(jax.ShapeDtypeStruct((PLANE, 8, 512), f32), jax.ShapeDtypeStruct((R, R), f32)),
        in_specs=[pl.BlockSpec(memory_space=pl.ANY)],
        out_specs=(vmem, vmem),
        scratch_shapes=[
            pltpu.VMEM((R, 512), jnp.bfloat16),
            pltpu.VMEM((R, 512), jnp.bfloat16),
            pltpu.VMEM((2 * NX, NZ, *piece), f32),
            pltpu.VMEM((NX, NZ, *piece), f32),
            pltpu.VMEM((NX, NZ, *piece), f32),
            pltpu.VMEM((NZ, *piece), f32),
            pltpu.VMEM((NZ, *piece), f32),
            pltpu.VMEM(piece, f32),
            pltpu.VMEM((NY, *piece), f32),
            pltpu.VMEM((2, NX, NZ, *piece), f32),
            dma((2,)), dma((2, PLANE)), dma((2, PLANE)),
            dma((NX,)), dma((NX,)), dma((NX, NZ)), dma((NX, NZ)), dma((NZ,)), dma((NZ,)), dma((NY,)), dma((NY,)),
            dma((NZ,)), dma((NX, NZ)), dma((NX, NZ)), dma((2, NX, NZ)),
        ],
        compiler_params=pltpu.CompilerParams(
            collective_id=0, has_side_effects=True, vmem_limit_bytes=VM * 2**20),
    )(tensor)


def dot_full(a, b, da, db):
    return lax.dot_general(
        a, b, (((da,), (db,)), ((), ())), precision=precise, preferred_element_type=jnp.float32)


def row_of(tile, j):
    return jnp.broadcast_to(tile[j:j + 1, :], (8, N))


def column_of(tile, j):
    return jnp.broadcast_to(tile[:, j:j + 1], (8, N))


def split(a):
    high = a.astype(jnp.bfloat16)
    return high, (a - high.astype(jnp.float32)).astype(jnp.bfloat16)


def dot_split(a, b, da, db):
    (a_high, a_low), (b_high, b_low) = split(a), split(b)

    def dot(p, q):
        return lax.dot_general(p, q, (((da,), (db,)), ((), ())), preferred_element_type=jnp.float32)

    return dot(a_high, b_high) + (dot(a_high, b_low) + dot(a_low, b_high))


def factor(m_ref, u_ref, v_ref):
    line, lane = (lax.broadcasted_iota(jnp.int32, (8, N), d) for d in range(2))
    for first in range(0, N, 32):
        last = first + 32
        m = [m_ref[first + 8 * i:first + 8 * i + 8, :] for i in range(4)]
        for b in range(4):
            start = first + 8 * b
            stop = start + 8
            inside = (lane >= start) & (lane < stop)
            columns = {i: [column_of(m[i], start + k) for k in range(8)] for i in range(b, 4)}
            for i in range(b, 4):
                m[i] = jnp.where(inside, (lane - start == line).astype(jnp.float32) if i == b else 0.0, m[i])
            pivots = jnp.zeros((8, N), jnp.float32)
            for j in range(8):
                pivot = row_of(columns[b][j], j)
                inverse = 1.0 / pivot
                pivots = jnp.where(line == j, pivot, pivots)
                row = row_of(m[b], j)
                row_columns = {k: row_of(columns[b][k], j) for k in range(j + 1, 8)}
                for i in range(b, 4):
                    ratio = columns[i][j] * inverse
                    if i == b:
                        ratio = jnp.where(line > j, ratio, 0.0)
                    m[i] = m[i] - ratio * row
                    for k in range(j + 1, 8):
                        columns[i][k] = columns[i][k] - ratio * row_columns[k]
            root = lax.rsqrt(pivots)
            root = root * (1.5 - 0.5 * (pivots * root) * root)
            m[b] = m[b] * root
            corner = jnp.zeros((8, N), jnp.float32)
            for k in range(8):
                corner = jnp.where((lane == start + k) & (line <= k), columns[b][k], corner)
            u_ref[start:stop, :] = jnp.where(lane >= stop, m[b], corner * root)
            v_ref[start:stop, :] = jnp.where(lane < stop, m[b], 0.0)
        if last < N:
            done = jnp.concatenate(m, axis=0)
            left = done.T[last:, :]
            right = jnp.concatenate(
                [jnp.where((lane >= first + 8 * b + 8) & (lane < last), 0.0, m[b]) for b in range(4)], axis=0)
            update = dot_full(left, right, 1, 0)
            wide = lax.broadcasted_iota(jnp.int32, (N - last, N), 1)
            m_ref[last:, :] = jnp.where((wide >= first) & (wide < last), 0.0, m_ref[last:, :]) - update


def factor_kernel(g_ref, initial_ref, basis_ref, triangle_ref, rest_ref, high_ref, low_ref, m_ref, u_ref, v_ref):
    c = lax.rem(lax.axis_index("mode"), 2)

    @pl.when(c == 0)
    def _():
        rest_ref[...] = g_ref[...]
        triangle_ref[...] = jnp.zeros((R, R), jnp.float32)
        for k in range(4):
            own, after = pl.ds(k * N, N), pl.ds((k + 1) * N, R - (k + 1) * N)
            m_ref[...] = rest_ref[own, own]
            factor(m_ref, u_ref, v_ref)
            triangle_ref[own, own] = u_ref[...]
            if k < 3:
                panel = dot_split(v_ref[...], rest_ref[own, after], 1, 0)
                triangle_ref[own, after] = panel
                for i in range(k + 1, 4):
                    left = panel[:, (i - k - 1) * N:(i - k) * N]
                    right = panel[:, (i - k - 1) * N:]
                    rest_ref[pl.ds(i * N, N), pl.ds(i * N, R - i * N)] -= dot_split(left, right, 0, 0)

    @pl.when(c == 1)
    def _():
        high_ref[...], low_ref[...] = split(g_ref[...])
        basis_ref[...] = initial_ref[...]

        def sweep(step, carry):
            high, low = split(basis_ref[...])
            both = jnp.dot(high_ref[...], jnp.concatenate([high, low], axis=1), preferred_element_type=jnp.float32)
            product = both[:, :N] + (both[:, N:] + jnp.dot(low_ref[...], high, preferred_element_type=jnp.float32))
            basis_ref[...] = product
            m_ref[...] = dot_full(product, product, 0, 0)
            factor(m_ref, u_ref, v_ref)
            basis_ref[...] = dot_full(basis_ref[...], v_ref[...], 1, 1)
            return carry

        lax.fori_loop(0, ITERS, sweep, 0)


def factored(gram, initial):
    f32 = jnp.float32
    vmem = pl.BlockSpec(memory_space=pltpu.VMEM)
    square = pltpu.VMEM((N, N), f32)
    return pl.pallas_call(
        factor_kernel,
        out_shape=(jax.ShapeDtypeStruct((R, N), f32), jax.ShapeDtypeStruct((R, R), f32)),
        in_specs=[vmem, vmem],
        out_specs=(vmem, vmem),
        scratch_shapes=[
            pltpu.VMEM((R, R), f32), pltpu.VMEM((R, R), jnp.bfloat16), pltpu.VMEM((R, R), jnp.bfloat16), square, square, square],
        compiler_params=pltpu.CompilerParams(vmem_limit_bytes=16 * 2**20),
    )(gram, initial)


def exchange_kernel(basis_ref, triangle_ref, basis_out, triangle_out, send_sem, recv_sem):
    m, z = lax.axis_index("mode"), lax.axis_index("col")
    c = lax.rem(m, 2)
    partner = {"mode": m + 1 - 2 * c, "col": z}
    barrier = pltpu.get_barrier_semaphore()
    pl.semaphore_signal(barrier, inc=1, device_id=partner, device_id_type=MESH)
    pl.semaphore_wait(barrier, 1)

    def over(src, dst, k):
        return pltpu.make_async_remote_copy(
            src, dst, send_sem.at[k], recv_sem.at[k], device_id=partner, device_id_type=MESH)

    def upper(ref, k):
        return ref.at[pl.ds(k * N, N), pl.ds(k * N, R - k * N)]

    strips = [over(upper(triangle_ref, k), upper(triangle_out, k), k) for k in range(4)]
    whole = over(basis_ref, basis_out, 4)

    @pl.when(c == 0)
    def _():
        for strip in strips:
            strip.start()
        triangle_out[...] = triangle_ref[...]
        whole.wait_recv()
        for strip in strips:
            strip.wait_send()

    @pl.when(c == 1)
    def _():
        whole.start()
        basis_out[...] = basis_ref[...]
        for k in range(1, 4):
            triangle_out[pl.ds(k * N, N), pl.ds(0, k * N)] = jnp.zeros((N, k * N), jnp.float32)
        for strip in strips:
            strip.wait_recv()
        whole.wait_send()


def exchanged(basis, triangle):
    dma = pltpu.SemaphoreType.DMA
    vmem = pl.BlockSpec(memory_space=pltpu.VMEM)
    return pl.pallas_call(
        exchange_kernel,
        out_shape=tuple(jax.ShapeDtypeStruct(a.shape, a.dtype) for a in (basis, triangle)),
        in_specs=[vmem, vmem],
        out_specs=(vmem, vmem),
        scratch_shapes=[dma((5,)), dma((5,))],
        compiler_params=pltpu.CompilerParams(
            collective_id=1, has_side_effects=True, vmem_limit_bytes=8 * 2**20),
    )(basis, triangle)


def core_kernel(basis_ref, triangle_ref, blocks_ref, core_ref, basis_out, triangle_out, sem):
    copies = [
        pltpu.make_async_copy(triangle_ref, triangle_out, sem.at[0]),
        pltpu.make_async_copy(basis_ref, basis_out, sem.at[1]),
    ]
    for copy in copies:
        copy.start()
    unfold = blocks_ref[...].reshape(R, 512)
    core = dot_full(basis_ref[...], unfold, 0, 0)
    for s in range(2):
        core_ref[:, s, :] = core[:, s * 256:(s + 1) * 256]
    for copy in copies:
        copy.wait()


def projected(basis, triangle, blocks):
    vmem, anywhere = (pl.BlockSpec(memory_space=space) for space in (pltpu.VMEM, pl.ANY))
    return pl.pallas_call(
        core_kernel,
        out_shape=tuple(jax.ShapeDtypeStruct(shape, jnp.float32) for shape in ((N, 2, 256), (R, N), (R, R))),
        in_specs=[vmem] * 3,
        out_specs=(vmem, anywhere, anywhere),
        scratch_shapes=[pltpu.SemaphoreType.DMA((2,))],
        compiler_params=pltpu.CompilerParams(vmem_limit_bytes=16 * 2**20),
    )(basis, triangle, blocks)


def local(tensor, initial):
    blocks, gram = gathered(tensor)
    basis, triangle = exchanged(*factored(gram, initial))
    return projected(basis, triangle, blocks)


def solution(mesh):
    return jax.shard_map(
        local,
        mesh=mesh,
        in_specs=(P("mode", "col", None), P()),
        out_specs=(P(None, "col", "mode"), P(), P()),
        check_vma=False,
    )
```

```python
import functools

import jax
import jax.numpy as jnp
from jax import lax
from jax.experimental import pallas as pl
from jax.experimental.pallas import tpu as pltpu
from jax.sharding import PartitionSpec as P

MESH = pl.DeviceIdType.MESH
ITERS = 3
R = 512
NX, NY, NZ = 4, 8, 8
PLANE = 2 * NX * NY
STARTS = (0, 512, 896, 1152)
N = 128
precise = lax.Precision.HIGHEST


def dot_nt(a, b):
    return lax.dot_general(a, b, (((1,), (1,)), ((), ())), preferred_element_type=jnp.float32)


def gather_kernel(t_ref, unf_ref, g_ref, hi, lo, gp, rc, rx, a2, rz, a3, ry, full,
                  own_sem, s_a2a, r_a2a, s_c, r_c, s_x, r_x, s_z, r_z, s_y, r_y,
                  s_fz, s_fx, s_fc, r_fc, r_full):
    m, z = lax.axis_index("mode"), lax.axis_index("col")
    c = lax.rem(m, 2)
    x = lax.rem(m // 2, NX)
    y = m // (2 * NX)

    def index(yy, xx, cc):
        return (yy * NX + xx) * 2 + cc

    def remote(src, dst, send_sem, recv_sem, mode, col):
        return pltpu.make_async_remote_copy(
            src, dst, send_sem, recv_sem, device_id={"mode": mode, "col": col}, device_id_type=MESH)

    def near(dy, dx, dc):
        return index(lax.rem(y + dy, NY), lax.rem(x + dx, NX), lax.rem(c + dc, 2))

    barrier = pltpu.get_barrier_semaphore()

    def greet(mode, col):
        pl.semaphore_signal(barrier, inc=1, device_id={"mode": mode, "col": col}, device_id_type=MESH)

    def greet_far(k, carry):
        for dy in (4, 3, 5, 2, 6, 1, 7, 0):
            greet(near(dy, k // 2, lax.rem(k, 2)), z)
        return carry

    for k in (4, 3, 5, 2, 6, 1, 7):
        greet(m, lax.rem(z + k, NZ))
    lax.fori_loop(1, 2 * NX, greet_far, 0)
    for dy in (4, 3, 5, 2, 6, 1, 7):
        greet(near(dy, 0, 0), z)
    pl.semaphore_wait(barrier, PLANE - 1 + NZ - 1)

    def columns(d, s):
        return t_ref.at[:, s, pl.ds(pl.multiple_of(d * 256, 256), 256)]

    def slab(src, s):
        return unf_ref.at[src, :, pl.ds(s * 256, 256)]

    def straight(d, src, s):
        return remote(columns(d, s), slab(src, s), s_a2a.at[s, d], r_a2a.at[s, src], d, z)

    def send(k, carry):
        for dy in (4, 1, 7, 2, 6, 3, 5, 0):
            for s in range(2):
                straight(near(dy, k // 2, lax.rem(k, 2)), m, s).start()
        return carry

    for dy in (4, 1, 7, 2, 6, 3, 5):
        for s in range(2):
            straight(near(dy, 0, 0), m, s).start()
    lax.fori_loop(1, 2 * NX, send, 0)
    own = [pltpu.make_async_copy(columns(m, s), slab(m, s), own_sem.at[s]) for s in range(2)]
    for copy in own:
        copy.start()
    for copy in own:
        copy.wait()

    def arrived(k, carry):
        d = lax.rem(m + k, PLANE)
        for s in range(2):
            straight(d, d, s).wait()
        return carry

    lax.fori_loop(1, PLANE, arrived, 0)

    unfold = unf_ref[...].reshape(R, 512)
    high = unfold.astype(jnp.bfloat16)
    hi[...] = high
    lo[...] = (unfold - high.astype(jnp.float32)).astype(jnp.bfloat16)
    scale = 1.0 / (512 * PLANE * NZ)
    gp[...] = jnp.zeros_like(gp)
    for i in range(4):
        h = hi[pl.ds(i * N, N), :]
        l = lo[pl.ds(i * N, N), :]
        rest = pl.ds(i * N, R - i * N)
        part = (dot_nt(h, hi[rest, :]) + (dot_nt(h, lo[rest, :]) + dot_nt(l, hi[rest, :]))) * scale
        for j in range(4 - i):
            tile = part[:, j * N:(j + 1) * N].reshape(8, 2, 8, N)
            q, lane = divmod(STARTS[i] // N + j, 3)
            for rg in range(2):
                gp[:, rg * 4 + q, :, lane * N:(lane + 1) * N] = tile[:, rg]

    def c_copy(to):
        return remote(gp.at[(1 - c) * NX + to], rc.at[to], s_c.at[to], r_c.at[to], index(y, x, 1 - c), z)

    ring_x = [lax.rem(x + k, NX) for k in (2, 1, 3, 0)]
    ring_z = [lax.rem(z + k, NZ) for k in (4, 3, 5, 2, 6, 1, 7)]
    for to in ring_x:
        c_copy(to).start()
    for to in ring_x:
        c_copy(to).wait()
        rc[to] += gp[c * NX + to]

    def x_copy(to, piece, src):
        return remote(rc.at[to, piece], rx.at[src, piece], s_x.at[to, piece], r_x.at[src, piece], index(y, to, c), z)

    def z_copy(to, src):
        return remote(a2.at[to], rz.at[src], s_z.at[to], r_z.at[src], m, to)

    for piece in ring_z + [z]:
        for to in ring_x[:3]:
            x_copy(to, piece, x).start()
    rx[x] = rc[x]
    for piece in ring_z + [z]:
        for to in ring_x[:3]:
            x_copy(to, piece, to).wait_recv()
        a2[piece] = (rx[0, piece] + rx[1, piece]) + (rx[2, piece] + rx[3, piece])
        if piece is not z:
            z_copy(piece, z).start()
    rz[z] = a2[z]
    for to in reversed(ring_z):
        z_copy(to, to).wait()
    a3[...] = ((rz[0] + rz[1]) + (rz[2] + rz[3])) + ((rz[4] + rz[5]) + (rz[6] + rz[7]))

    def y_copy(to, src):
        return remote(a3, ry.at[src], s_y.at[to], r_y.at[src], index(to, x, c), z)

    ring_y = [lax.rem(y + k, NY) for k in (4, 3, 5, 2, 6, 1, 7)]
    for to in ring_y:
        y_copy(to, y).start()
    ry[y] = a3[...]
    for to in reversed(ring_y):
        y_copy(to, to).wait()
    full[c, x, z] = ((ry[0] + ry[1]) + (ry[2] + ry[3])) + ((ry[4] + ry[5]) + (ry[6] + ry[7]))

    def fz_copy(to, src):
        return remote(full.at[c, x, src], full.at[c, x, src], s_fz.at[to], r_full.at[c, x, src], m, to)

    def fx_copy(to, src, piece):
        return remote(full.at[c, src, piece], full.at[c, src, piece], s_fx.at[to, piece], r_full.at[c, src, piece], index(y, to, c), z)

    def fc_copy(cc, piece):
        return remote(full.at[cc, :, piece], full.at[cc, :, piece], s_fc.at[piece], r_fc.at[piece], index(y, x, 1 - c), z)

    def pass_on(piece):
        for to in ring_x[:3]:
            fx_copy(to, x, piece).start()

    for to in ring_z:
        fz_copy(to, z).start()
    pass_on(z)
    for src in reversed(ring_z):
        fz_copy(src, src).wait_recv()
        pass_on(src)
    for piece in [z] + ring_z[::-1]:
        for src in (ring_x[1], ring_x[2], ring_x[0]):
            fx_copy(src, src, piece).wait_recv()
        fc_copy(c, piece).start()
    for piece in [z] + ring_z[::-1]:
        fc_copy(1 - c, piece).wait_recv()

    whole = full[...].reshape(16, 4, 8, 384)
    for i in range(4):
        for j in range(i, 4):
            q, lane = divmod(STARTS[i] // N + j - i, 3)
            block = whole[:, q, :, lane * N:(lane + 1) * N].reshape(N, N)
            g_ref[pl.ds(i * N, N), pl.ds(j * N, N)] = block
            if i != j:
                g_ref[pl.ds(j * N, N), pl.ds(i * N, N)] = block.T

    def sent_x(k, carry):
        for to in ring_x[:3]:
            x_copy(to, k, x).wait_send()
            fx_copy(to, x, k).wait_send()
        fc_copy(c, k).wait_send()
        return carry

    lax.fori_loop(0, NZ, sent_x, 0)
    for to in ring_z:
        fz_copy(to, z).wait_send()


def gathered(tensor):
    f32 = jnp.float32
    dma = pltpu.SemaphoreType.DMA
    vmem = pl.BlockSpec(memory_space=pltpu.VMEM)
    piece = (8, 384)
    return pl.pallas_call(
        gather_kernel,
        out_shape=(jax.ShapeDtypeStruct((PLANE, 8, 512), f32), jax.ShapeDtypeStruct((R, R), f32)),
        in_specs=[pl.BlockSpec(memory_space=pltpu.HBM)],
        out_specs=(vmem, vmem),
        scratch_shapes=[
            pltpu.VMEM((R, 512), jnp.bfloat16),
            pltpu.VMEM((R, 512), jnp.bfloat16),
            pltpu.VMEM((2 * NX, NZ, *piece), f32),
            pltpu.VMEM((NX, NZ, *piece), f32),
            pltpu.VMEM((NX, NZ, *piece), f32),
            pltpu.VMEM((NZ, *piece), f32),
            pltpu.VMEM((NZ, *piece), f32),
            pltpu.VMEM(piece, f32),
            pltpu.VMEM((NY, *piece), f32),
            pltpu.VMEM((2, NX, NZ, *piece), f32),
            dma((2,)), dma((2, PLANE)), dma((2, PLANE)),
            dma((NX,)), dma((NX,)), dma((NX, NZ)), dma((NX, NZ)), dma((NZ,)), dma((NZ,)), dma((NY,)), dma((NY,)),
            dma((NZ,)), dma((NX, NZ)), dma((NZ,)), dma((NZ,)), dma((2, NX, NZ)),
        ],
        compiler_params=pltpu.CompilerParams(
            collective_id=0, has_side_effects=True, vmem_limit_bytes=40 * 2**20),
    )(pltpu.with_memory_space_constraint(tensor, pltpu.HBM))


def dot_full(a, b, da, db):
    return lax.dot_general(
        a, b, (((da,), (db,)), ((), ())), precision=precise, preferred_element_type=jnp.float32)


def row_of(tile, j):
    return jnp.broadcast_to(tile[j:j + 1, :], (8, N))


def column_of(tile, j):
    return jnp.broadcast_to(tile[:, j:j + 1], (8, N))


def split(a):
    high = a.astype(jnp.bfloat16)
    return high, (a - high.astype(jnp.float32)).astype(jnp.bfloat16)


def dot_split(a, b, da, db):
    (a_high, a_low), (b_high, b_low) = split(a), split(b)

    def dot(p, q):
        return lax.dot_general(p, q, (((da,), (db,)), ((), ())), preferred_element_type=jnp.float32)

    return dot(a_high, b_high) + (dot(a_high, b_low) + dot(a_low, b_high))


def factor(m_ref, u_ref, v_ref):
    line, lane = (lax.broadcasted_iota(jnp.int32, (8, N), d) for d in range(2))
    for first in range(0, N, 32):
        last = first + 32
        m = [m_ref[first + 8 * i:first + 8 * i + 8, :] for i in range(4)]
        for b in range(4):
            start = first + 8 * b
            stop = start + 8
            inside = (lane >= start) & (lane < stop)
            columns = {i: [column_of(m[i], start + k) for k in range(8)] for i in range(b, 4)}
            for i in range(b, 4):
                m[i] = jnp.where(inside, (lane - start == line).astype(jnp.float32) if i == b else 0.0, m[i])
            pivots = jnp.zeros((8, N), jnp.float32)
            for j in range(0, 8, 2):
                row_columns = {k: row_of(columns[b][k], j) for k in range(j, 8)}
                pivot, beside = row_columns[j], row_columns[j + 1]
                square = pivot * row_of(columns[b][j + 1], j + 1) - beside * beside
                inverse, later = 1.0 / pivot, pivot * (1.0 / square)
                pivots = jnp.where(line == j, pivot, pivots)
                row = row_of(m[b], j)
                for i in range(b, 4):
                    ratio = columns[i][j] * inverse
                    if i == b:
                        ratio = jnp.where(line > j, ratio, 0.0)
                    m[i] = m[i] - ratio * row
                    for k in range(j + 1, 8):
                        columns[i][k] = columns[i][k] - ratio * row_columns[k]
                row_columns = {k: row_of(columns[b][k], j + 1) for k in range(j + 1, 8)}
                pivots = jnp.where(line == j + 1, row_columns[j + 1], pivots)
                row = row_of(m[b], j + 1)
                for i in range(b, 4):
                    ratio = columns[i][j + 1] * later
                    if i == b:
                        ratio = jnp.where(line > j + 1, ratio, 0.0)
                    m[i] = m[i] - ratio * row
                    for k in range(j + 2, 8):
                        columns[i][k] = columns[i][k] - ratio * row_columns[k]
            root = lax.rsqrt(pivots)
            root = root * (1.5 - 0.5 * (pivots * root) * root)
            m[b] = m[b] * root
            corner = jnp.zeros((8, N), jnp.float32)
            for k in range(8):
                corner = jnp.where((lane == start + k) & (line <= k), columns[b][k], corner)
            u_ref[start:stop, :] = jnp.where(lane >= stop, m[b], corner * root)
            v_ref[start:stop, :] = jnp.where(lane < stop, m[b], 0.0)
        if last < N:
            done = jnp.concatenate(m, axis=0)
            left = done.T[last:, :]
            right = jnp.concatenate(
                [jnp.where((lane >= first + 8 * b + 8) & (lane < last), 0.0, m[b]) for b in range(4)], axis=0)
            update = dot_full(left, right, 1, 0)
            wide = lax.broadcasted_iota(jnp.int32, (N - last, N), 1)
            m_ref[last:, :] = jnp.where((wide >= first) & (wide < last), 0.0, m_ref[last:, :]) - update


def factor_kernel(g_ref, initial_ref, basis_ref, triangle_ref, rest_ref, high_ref, low_ref, m_ref, u_ref, v_ref):
    c = lax.rem(lax.axis_index("mode"), 2)

    @pl.when(c == 0)
    def _():
        rest_ref[...] = g_ref[...]
        triangle_ref[...] = jnp.zeros((R, R), jnp.float32)
        for k in range(4):
            own, after = pl.ds(k * N, N), pl.ds((k + 1) * N, R - (k + 1) * N)
            m_ref[...] = rest_ref[own, own]
            factor(m_ref, u_ref, v_ref)
            triangle_ref[own, own] = u_ref[...]
            if k < 3:
                panel = dot_split(v_ref[...], rest_ref[own, after], 1, 0)
                triangle_ref[own, after] = panel
                for i in range(k + 1, 4):
                    left = panel[:, (i - k - 1) * N:(i - k) * N]
                    right = panel[:, (i - k - 1) * N:]
                    rest_ref[pl.ds(i * N, N), pl.ds(i * N, R - i * N)] -= dot_split(left, right, 0, 0)

    @pl.when(c == 1)
    def _():
        high_ref[...], low_ref[...] = split(g_ref[...])
        basis_ref[...] = initial_ref[...]

        def sweep(step, carry):
            high, low = split(basis_ref[...])
            both = jnp.dot(high_ref[...], jnp.concatenate([high, low], axis=1), preferred_element_type=jnp.float32)
            product = both[:, :N] + (both[:, N:] + jnp.dot(low_ref[...], high, preferred_element_type=jnp.float32))
            basis_ref[...] = product
            m_ref[...] = dot_full(product, product, 0, 0)
            factor(m_ref, u_ref, v_ref)
            basis_ref[...] = dot_full(basis_ref[...], v_ref[...], 1, 1)
            return carry

        lax.fori_loop(0, ITERS, sweep, 0)


def factored(gram, initial):
    f32 = jnp.float32
    vmem = pl.BlockSpec(memory_space=pltpu.VMEM)
    square = pltpu.VMEM((N, N), f32)
    return pl.pallas_call(
        factor_kernel,
        out_shape=(jax.ShapeDtypeStruct((R, N), f32), jax.ShapeDtypeStruct((R, R), f32)),
        in_specs=[vmem, vmem],
        out_specs=(vmem, vmem),
        scratch_shapes=[
            pltpu.VMEM((R, R), f32), pltpu.VMEM((R, R), jnp.bfloat16), pltpu.VMEM((R, R), jnp.bfloat16), square, square, square],
        compiler_params=pltpu.CompilerParams(vmem_limit_bytes=16 * 2**20),
    )(gram, initial)


def exchange_kernel(basis_ref, triangle_ref, basis_out, triangle_out, send_sem, recv_sem):
    m, z = lax.axis_index("mode"), lax.axis_index("col")
    c = lax.rem(m, 2)
    partner = {"mode": m + 1 - 2 * c, "col": z}
    barrier = pltpu.get_barrier_semaphore()
    pl.semaphore_signal(barrier, inc=1, device_id=partner, device_id_type=MESH)
    pl.semaphore_wait(barrier, 1)

    def over(src, dst, k):
        return pltpu.make_async_remote_copy(
            src, dst, send_sem.at[k], recv_sem.at[k], device_id=partner, device_id_type=MESH)

    def upper(ref, k):
        return ref.at[pl.ds(k * N, N), pl.ds(k * N, R - k * N)]

    strips = [over(upper(triangle_ref, k), upper(triangle_out, k), k) for k in range(4)]
    whole = over(basis_ref, basis_out, 4)

    @pl.when(c == 0)
    def _():
        for strip in strips:
            strip.start()
        triangle_out[...] = triangle_ref[...]
        whole.wait_recv()
        for strip in strips:
            strip.wait_send()

    @pl.when(c == 1)
    def _():
        whole.start()
        basis_out[...] = basis_ref[...]
        for k in range(1, 4):
            triangle_out[pl.ds(k * N, N), pl.ds(0, k * N)] = jnp.zeros((N, k * N), jnp.float32)
        for strip in strips:
            strip.wait_recv()
        whole.wait_send()


def exchanged(basis, triangle):
    dma = pltpu.SemaphoreType.DMA
    vmem = pl.BlockSpec(memory_space=pltpu.VMEM)
    return pl.pallas_call(
        exchange_kernel,
        out_shape=tuple(jax.ShapeDtypeStruct(a.shape, a.dtype) for a in (basis, triangle)),
        in_specs=[vmem, vmem],
        out_specs=(vmem, vmem),
        scratch_shapes=[dma((5,)), dma((5,))],
        compiler_params=pltpu.CompilerParams(
            collective_id=1, has_side_effects=True, vmem_limit_bytes=8 * 2**20),
    )(basis, triangle)


def core_kernel(basis_ref, triangle_ref, blocks_ref, core_ref, basis_out, triangle_out, sem):
    copies = [
        pltpu.make_async_copy(triangle_ref, triangle_out, sem.at[0]),
        pltpu.make_async_copy(basis_ref, basis_out, sem.at[1]),
    ]
    for copy in copies:
        copy.start()
    unfold = blocks_ref[...].reshape(R, 512)
    core = dot_split(basis_ref[...], unfold, 0, 0)
    for s in range(2):
        core_ref[:, s, :] = core[:, s * 256:(s + 1) * 256]
    for copy in copies:
        copy.wait()


def projected(basis, triangle, blocks):
    vmem, anywhere = (pl.BlockSpec(memory_space=space) for space in (pltpu.VMEM, pl.ANY))
    return pl.pallas_call(
        core_kernel,
        out_shape=tuple(jax.ShapeDtypeStruct(shape, jnp.float32) for shape in ((N, 2, 256), (R, N), (R, R))),
        in_specs=[vmem] * 3,
        out_specs=(vmem, anywhere, anywhere),
        scratch_shapes=[pltpu.SemaphoreType.DMA((2,))],
        compiler_params=pltpu.CompilerParams(vmem_limit_bytes=16 * 2**20),
    )(basis, triangle, blocks)


def local(tensor, initial):
    blocks, gram = gathered(tensor)
    basis, triangle = exchanged(*factored(gram, initial))
    return projected(basis, triangle, blocks)


def solution(mesh):
    return jax.shard_map(
        local,
        mesh=mesh,
        in_specs=(P("mode", "col", None), P()),
        out_specs=(P(None, "col", "mode"), P(), P()),
        check_vma=False,
    )
```

```python
import functools

import jax
import jax.numpy as jnp
from jax import lax
from jax.experimental import pallas as pl
from jax.experimental.pallas import tpu as pltpu
from jax.sharding import PartitionSpec as P

MESH = pl.DeviceIdType.MESH
ITERS = 3
R = 512
NX, NY, NZ = 4, 8, 8
PLANE = 2 * NX * NY
STARTS = (0, 512, 896, 1152)
N = 128
precise = lax.Precision.HIGHEST


def dot_nt(a, b):
    return lax.dot_general(a, b, (((1,), (1,)), ((), ())), preferred_element_type=jnp.float32)


def gather_kernel(t_ref, unf_ref, g_ref, hi, lo, gp, rc, rx, a2, rz, a3, ry, full,
                  own_sem, s_a2a, r_a2a, s_c, r_c, s_x, r_x, s_z, r_z, s_y, r_y,
                  s_fz, s_fx, s_fc, r_fc, r_full):
    m, z = lax.axis_index("mode"), lax.axis_index("col")
    c = lax.rem(m, 2)
    x = lax.rem(m // 2, NX)
    y = m // (2 * NX)

    def index(yy, xx, cc):
        return (yy * NX + xx) * 2 + cc

    def remote(src, dst, send_sem, recv_sem, mode, col):
        return pltpu.make_async_remote_copy(
            src, dst, send_sem, recv_sem, device_id={"mode": mode, "col": col}, device_id_type=MESH)

    def near(dy, dx, dc):
        return index(lax.rem(y + dy, NY), lax.rem(x + dx, NX), lax.rem(c + dc, 2))

    barrier = pltpu.get_barrier_semaphore()

    def greet(mode, col):
        pl.semaphore_signal(barrier, inc=1, device_id={"mode": mode, "col": col}, device_id_type=MESH)

    def greet_far(k, carry):
        for dy in (4, 3, 5, 2, 6, 1, 7, 0):
            greet(near(dy, k // 2, lax.rem(k, 2)), z)
        return carry

    for k in (4, 3, 5, 2, 6, 1, 7):
        greet(m, lax.rem(z + k, NZ))
    lax.fori_loop(1, 2 * NX, greet_far, 0)
    for dy in (4, 3, 5, 2, 6, 1, 7):
        greet(near(dy, 0, 0), z)
    pl.semaphore_wait(barrier, PLANE - 1 + NZ - 1)

    def columns(d, s):
        return t_ref.at[:, s, pl.ds(pl.multiple_of(d * 256, 256), 256)]

    def slab(src, s):
        return unf_ref.at[src, :, pl.ds(s * 256, 256)]

    def straight(d, src, s):
        return remote(columns(d, s), slab(src, s), s_a2a.at[s, d], r_a2a.at[s, src], d, z)

    def send(k, carry):
        for dy in (4, 1, 7, 2, 6, 3, 5, 0):
            for s in range(2):
                straight(near(dy, k // 2, lax.rem(k, 2)), m, s).start()
        return carry

    for dy in (4, 1, 7, 2, 6, 3, 5):
        for s in range(2):
            straight(near(dy, 0, 0), m, s).start()
    lax.fori_loop(1, 2 * NX, send, 0)
    own = [pltpu.make_async_copy(columns(m, s), slab(m, s), own_sem.at[s]) for s in range(2)]
    for copy in own:
        copy.start()
    for copy in own:
        copy.wait()

    def arrived(k, carry):
        d = lax.rem(m + k, PLANE)
        for s in range(2):
            straight(d, d, s).wait()
        return carry

    lax.fori_loop(1, PLANE, arrived, 0)

    unfold = unf_ref[...].reshape(R, 512)
    high = unfold.astype(jnp.bfloat16)
    hi[...] = high
    lo[...] = (unfold - high.astype(jnp.float32)).astype(jnp.bfloat16)
    scale = 1.0 / (512 * PLANE * NZ)
    gp[...] = jnp.zeros_like(gp)
    for i in range(4):
        h = hi[pl.ds(i * N, N), :]
        l = lo[pl.ds(i * N, N), :]
        rest = pl.ds(i * N, R - i * N)
        part = (dot_nt(h, hi[rest, :]) + (dot_nt(h, lo[rest, :]) + dot_nt(l, hi[rest, :]))) * scale
        for j in range(4 - i):
            tile = part[:, j * N:(j + 1) * N].reshape(8, 2, 8, N)
            q, lane = divmod(STARTS[i] // N + j, 3)
            for rg in range(2):
                gp[:, rg * 4 + q, :, lane * N:(lane + 1) * N] = tile[:, rg]

    def c_copy(to):
        return remote(gp.at[(1 - c) * NX + to], rc.at[to], s_c.at[to], r_c.at[to], index(y, x, 1 - c), z)

    ring_x = [lax.rem(x + k, NX) for k in (2, 1, 3, 0)]
    ring_z = [lax.rem(z + k, NZ) for k in (4, 3, 5, 2, 6, 1, 7)]
    for to in ring_x:
        c_copy(to).start()
    for to in ring_x:
        c_copy(to).wait()
        rc[to] += gp[c * NX + to]

    def fitting(piece, act):
        for last in (False, True):
            width = N if last else 3 * N

            @pl.when((lax.rem(piece, 4) == 3) == last)
            def _():
                act(pl.ds(0, width))

    def x_copy(to, piece, src, lanes):
        return remote(rc.at[to, piece, :, lanes], rx.at[src, piece, :, lanes], s_x.at[to, piece], r_x.at[src, piece], index(y, to, c), z)

    def z_copy(to, src):
        return remote(a2.at[to], rz.at[src], s_z.at[to], r_z.at[src], m, to)

    for piece in ring_z + [z]:
        fitting(piece, lambda lanes: [x_copy(to, piece, x, lanes).start() for to in ring_x[:3]])
    rx[x] = rc[x]
    for piece in ring_z + [z]:
        fitting(piece, lambda lanes: [x_copy(to, piece, to, lanes).wait_recv() for to in ring_x[:3]])
        a2[piece] = (rx[0, piece] + rx[1, piece]) + (rx[2, piece] + rx[3, piece])
        if piece is not z:
            z_copy(piece, z).start()
    rz[z] = a2[z]
    for to in reversed(ring_z):
        z_copy(to, to).wait()
    a3[...] = ((rz[0] + rz[1]) + (rz[2] + rz[3])) + ((rz[4] + rz[5]) + (rz[6] + rz[7]))

    def y_copy(to, src):
        return remote(a3, ry.at[src], s_y.at[to], r_y.at[src], index(to, x, c), z)

    ring_y = [lax.rem(y + k, NY) for k in (4, 3, 5, 2, 6, 1, 7)]
    for to in ring_y:
        y_copy(to, y).start()
    ry[y] = a3[...]
    for to in reversed(ring_y):
        y_copy(to, to).wait()
    full[c, x, z] = ((ry[0] + ry[1]) + (ry[2] + ry[3])) + ((ry[4] + ry[5]) + (ry[6] + ry[7]))

    def fz_copy(to, src):
        return remote(full.at[c, x, src], full.at[c, x, src], s_fz.at[to], r_full.at[c, x, src], m, to)

    def fx_copy(to, src, piece, lanes):
        part = full.at[c, src, piece, :, lanes]
        return remote(part, part, s_fx.at[to, piece], r_full.at[c, src, piece], index(y, to, c), z)

    def fc_copy(cc, piece):
        return remote(full.at[cc, :, piece], full.at[cc, :, piece], s_fc.at[piece], r_fc.at[piece], index(y, x, 1 - c), z)

    def pass_on(piece):
        fitting(piece, lambda lanes: [fx_copy(to, x, piece, lanes).start() for to in ring_x[:3]])

    for to in ring_z:
        fz_copy(to, z).start()
    pass_on(z)
    for src in reversed(ring_z):
        fz_copy(src, src).wait_recv()
        pass_on(src)
    for piece in [z] + ring_z[::-1]:
        fitting(piece, lambda lanes: [fx_copy(src, src, piece, lanes).wait_recv() for src in ring_x[:3]])
        fc_copy(c, piece).start()
    for piece in [z] + ring_z[::-1]:
        fc_copy(1 - c, piece).wait_recv()

    whole = full[...].reshape(16, 4, 8, 384)
    for i in range(4):
        for j in range(i, 4):
            q, lane = divmod(STARTS[i] // N + j - i, 3)
            block = whole[:, q, :, lane * N:(lane + 1) * N].reshape(N, N)
            g_ref[pl.ds(i * N, N), pl.ds(j * N, N)] = block
            if i != j:
                g_ref[pl.ds(j * N, N), pl.ds(i * N, N)] = block.T

    def sent_x(k, carry):
        fitting(k, lambda lanes: [copy.wait_send() for to in ring_x[:3] for copy in (x_copy(to, k, x, lanes), fx_copy(to, x, k, lanes))])
        fc_copy(c, k).wait_send()
        return carry

    lax.fori_loop(0, NZ, sent_x, 0)
    for to in ring_z:
        fz_copy(to, z).wait_send()


def gathered(tensor):
    f32 = jnp.float32
    dma = pltpu.SemaphoreType.DMA
    vmem = pl.BlockSpec(memory_space=pltpu.VMEM)
    piece = (8, 384)
    return pl.pallas_call(
        gather_kernel,
        out_shape=(jax.ShapeDtypeStruct((PLANE, 8, 512), f32), jax.ShapeDtypeStruct((R, R), f32)),
        in_specs=[pl.BlockSpec(memory_space=pltpu.HBM)],
        out_specs=(vmem, vmem),
        scratch_shapes=[
            pltpu.VMEM((R, 512), jnp.bfloat16),
            pltpu.VMEM((R, 512), jnp.bfloat16),
            pltpu.VMEM((2 * NX, NZ, *piece), f32),
            pltpu.VMEM((NX, NZ, *piece), f32),
            pltpu.VMEM((NX, NZ, *piece), f32),
            pltpu.VMEM((NZ, *piece), f32),
            pltpu.VMEM((NZ, *piece), f32),
            pltpu.VMEM(piece, f32),
            pltpu.VMEM((NY, *piece), f32),
            pltpu.VMEM((2, NX, NZ, *piece), f32),
            dma((2,)), dma((2, PLANE)), dma((2, PLANE)),
            dma((NX,)), dma((NX,)), dma((NX, NZ)), dma((NX, NZ)), dma((NZ,)), dma((NZ,)), dma((NY,)), dma((NY,)),
            dma((NZ,)), dma((NX, NZ)), dma((NZ,)), dma((NZ,)), dma((2, NX, NZ)),
        ],
        compiler_params=pltpu.CompilerParams(
            collective_id=0, has_side_effects=True, vmem_limit_bytes=40 * 2**20),
    )(pltpu.with_memory_space_constraint(tensor, pltpu.HBM))


def dot_full(a, b, da, db):
    return lax.dot_general(
        a, b, (((da,), (db,)), ((), ())), precision=precise, preferred_element_type=jnp.float32)


def row_of(tile, j):
    return jnp.broadcast_to(tile[j:j + 1, :], (8, N))


def column_of(tile, j):
    return jnp.broadcast_to(tile[:, j:j + 1], (8, N))


def split(a):
    high = a.astype(jnp.bfloat16)
    return high, (a - high.astype(jnp.float32)).astype(jnp.bfloat16)


def dot_split(a, b, da, db):
    (a_high, a_low), (b_high, b_low) = split(a), split(b)

    def dot(p, q):
        return lax.dot_general(p, q, (((da,), (db,)), ((), ())), preferred_element_type=jnp.float32)

    return dot(a_high, b_high) + (dot(a_high, b_low) + dot(a_low, b_high))


def factor(m_ref, u_ref, v_ref):
    line, lane = (lax.broadcasted_iota(jnp.int32, (8, N), d) for d in range(2))
    for first in range(0, N, 32):
        last = first + 32
        m = [m_ref[first + 8 * i:first + 8 * i + 8, :] for i in range(4)]
        for b in range(4):
            start = first + 8 * b
            stop = start + 8
            inside = (lane >= start) & (lane < stop)
            columns = {i: [column_of(m[i], start + k) for k in range(8)] for i in range(b, 4)}
            for i in range(b, 4):
                m[i] = jnp.where(inside, (lane - start == line).astype(jnp.float32) if i == b else 0.0, m[i])
            pivots = jnp.zeros((8, N), jnp.float32)
            for j in range(0, 8, 2):
                row_columns = {k: row_of(columns[b][k], j) for k in range(j, 8)}
                pivot, beside = row_columns[j], row_columns[j + 1]
                square = pivot * row_of(columns[b][j + 1], j + 1) - beside * beside
                inverse, later = 1.0 / pivot, pivot * (1.0 / square)
                pivots = jnp.where(line == j, pivot, pivots)
                row = row_of(m[b], j)
                for i in range(b, 4):
                    ratio = columns[i][j] * inverse
                    if i == b:
                        ratio = jnp.where(line > j, ratio, 0.0)
                    m[i] = m[i] - ratio * row
                    for k in range(j + 1, 8):
                        columns[i][k] = columns[i][k] - ratio * row_columns[k]
                row_columns = {k: row_of(columns[b][k], j + 1) for k in range(j + 1, 8)}
                pivots = jnp.where(line == j + 1, row_columns[j + 1], pivots)
                row = row_of(m[b], j + 1)
                for i in range(b, 4):
                    ratio = columns[i][j + 1] * later
                    if i == b:
                        ratio = jnp.where(line > j + 1, ratio, 0.0)
                    m[i] = m[i] - ratio * row
                    for k in range(j + 2, 8):
                        columns[i][k] = columns[i][k] - ratio * row_columns[k]
            root = lax.rsqrt(pivots)
            root = root * (1.5 - 0.5 * (pivots * root) * root)
            m[b] = m[b] * root
            corner = jnp.zeros((8, N), jnp.float32)
            for k in range(8):
                corner = jnp.where((lane == start + k) & (line <= k), columns[b][k], corner)
            u_ref[start:stop, :] = jnp.where(lane >= stop, m[b], corner * root)
            v_ref[start:stop, :] = jnp.where(lane < stop, m[b], 0.0)
        if last < N:
            done = jnp.concatenate(m, axis=0)
            left = done.T[last:, :]
            right = jnp.concatenate(
                [jnp.where((lane >= first + 8 * b + 8) & (lane < last), 0.0, m[b]) for b in range(4)], axis=0)
            update = dot_full(left, right, 1, 0)
            wide = lax.broadcasted_iota(jnp.int32, (N - last, N), 1)
            m_ref[last:, :] = jnp.where((wide >= first) & (wide < last), 0.0, m_ref[last:, :]) - update


def factor_kernel(g_ref, initial_ref, basis_ref, triangle_ref, rest_ref, high_ref, low_ref, m_ref, u_ref, v_ref):
    c = lax.rem(lax.axis_index("mode"), 2)

    @pl.when(c == 0)
    def _():
        for k in range(4):
            own, after = pl.ds(k * N, N), pl.ds((k + 1) * N, R - (k + 1) * N)
            left_ref = rest_ref if k else g_ref
            m_ref[...] = left_ref[own, own]
            if k:
                triangle_ref[own, pl.ds(0, k * N)] = jnp.zeros((N, k * N), jnp.float32)
            factor(m_ref, u_ref, v_ref)
            triangle_ref[own, own] = u_ref[...]
            if k < 3:
                panel = dot_split(v_ref[...], left_ref[own, after], 1, 0)
                triangle_ref[own, after] = panel
                for i in range(k + 1, 4):
                    left = panel[:, (i - k - 1) * N:(i - k) * N]
                    right = panel[:, (i - k - 1) * N:]
                    there = pl.ds(i * N, N), pl.ds(i * N, R - i * N)
                    rest_ref[there] = left_ref[there] - dot_split(left, right, 0, 0)

    @pl.when(c == 1)
    def _():
        high_ref[...], low_ref[...] = split(g_ref[...])
        basis_ref[...] = initial_ref[...]

        def sweep(step, carry):
            high, low = split(basis_ref[...])
            both = jnp.dot(high_ref[...], jnp.concatenate([high, low], axis=1), preferred_element_type=jnp.float32)
            product = both[:, :N] + (both[:, N:] + jnp.dot(low_ref[...], high, preferred_element_type=jnp.float32))
            basis_ref[...] = product
            m_ref[...] = dot_full(product, product, 0, 0)
            factor(m_ref, u_ref, v_ref)
            basis_ref[...] = dot_full(basis_ref[...], v_ref[...], 1, 1)
            return carry

        lax.fori_loop(0, ITERS, sweep, 0)


def factored(gram, initial):
    f32 = jnp.float32
    vmem = pl.BlockSpec(memory_space=pltpu.VMEM)
    square = pltpu.VMEM((N, N), f32)
    return pl.pallas_call(
        factor_kernel,
        out_shape=(jax.ShapeDtypeStruct((R, N), f32), jax.ShapeDtypeStruct((R, R), f32)),
        in_specs=[vmem, vmem],
        out_specs=(vmem, vmem),
        scratch_shapes=[
            pltpu.VMEM((R, R), f32), pltpu.VMEM((R, R), jnp.bfloat16), pltpu.VMEM((R, R), jnp.bfloat16), square, square, square],
        compiler_params=pltpu.CompilerParams(vmem_limit_bytes=16 * 2**20),
    )(gram, initial)


def exchange_kernel(basis_ref, triangle_ref, basis_out, triangle_out, send_sem, recv_sem):
    m, z = lax.axis_index("mode"), lax.axis_index("col")
    c = lax.rem(m, 2)
    partner = {"mode": m + 1 - 2 * c, "col": z}
    barrier = pltpu.get_barrier_semaphore()
    pl.semaphore_signal(barrier, inc=1, device_id=partner, device_id_type=MESH)
    pl.semaphore_wait(barrier, 1)

    def over(src, dst, k):
        return pltpu.make_async_remote_copy(
            src, dst, send_sem.at[k], recv_sem.at[k], device_id=partner, device_id_type=MESH)

    def upper(ref, k):
        return ref.at[pl.ds(k * N, N), pl.ds(k * N, R - k * N)]

    strips = [over(upper(triangle_ref, k), upper(triangle_out, k), k) for k in range(4)]
    whole = over(basis_ref, basis_out, 4)

    @pl.when(c == 0)
    def _():
        for strip in strips:
            strip.start()
        triangle_out[...] = triangle_ref[...]
        whole.wait_recv()
        for strip in strips:
            strip.wait_send()

    @pl.when(c == 1)
    def _():
        whole.start()
        basis_out[...] = basis_ref[...]
        for k in range(1, 4):
            triangle_out[pl.ds(k * N, N), pl.ds(0, k * N)] = jnp.zeros((N, k * N), jnp.float32)
        for strip in strips:
            strip.wait_recv()
        whole.wait_send()


def exchanged(basis, triangle):
    dma = pltpu.SemaphoreType.DMA
    vmem = pl.BlockSpec(memory_space=pltpu.VMEM)
    return pl.pallas_call(
        exchange_kernel,
        out_shape=tuple(jax.ShapeDtypeStruct(a.shape, a.dtype) for a in (basis, triangle)),
        in_specs=[vmem, vmem],
        out_specs=(vmem, vmem),
        scratch_shapes=[dma((5,)), dma((5,))],
        compiler_params=pltpu.CompilerParams(
            collective_id=1, has_side_effects=True, vmem_limit_bytes=8 * 2**20),
    )(basis, triangle)


def core_kernel(basis_ref, triangle_ref, blocks_ref, core_out, basis_out, triangle_out, core_ref, sem):
    copies = [
        pltpu.make_async_copy(triangle_ref, triangle_out, sem.at[0]),
        pltpu.make_async_copy(basis_ref, basis_out, sem.at[1]),
    ]
    for copy in copies:
        copy.start()
    unfold = blocks_ref[...].reshape(R, 512)
    core = dot_split(basis_ref[...], unfold, 0, 0)
    for part in range(2):
        rows = pl.ds(part * 64, 64)
        for s in range(2):
            core_ref[rows, s, :] = core[part * 64:(part + 1) * 64, s * 256:(s + 1) * 256]
        copies.append(pltpu.make_async_copy(core_ref.at[rows], core_out.at[rows], sem.at[2 + part]))
        copies[-1].start()
    for copy in copies:
        copy.wait()


def projected(basis, triangle, blocks):
    vmem, anywhere = (pl.BlockSpec(memory_space=space) for space in (pltpu.VMEM, pl.ANY))
    return pl.pallas_call(
        core_kernel,
        out_shape=tuple(jax.ShapeDtypeStruct(shape, jnp.float32) for shape in ((N, 2, 256), (R, N), (R, R))),
        in_specs=[vmem] * 3,
        out_specs=(anywhere, anywhere, anywhere),
        scratch_shapes=[pltpu.VMEM((N, 2, 256), jnp.float32), pltpu.SemaphoreType.DMA((4,))],
        compiler_params=pltpu.CompilerParams(vmem_limit_bytes=16 * 2**20),
    )(basis, triangle, blocks)


def local(tensor, initial):
    blocks, gram = gathered(tensor)
    basis, triangle = exchanged(*factored(gram, initial))
    return projected(basis, triangle, blocks)


def solution(mesh):
    return jax.shard_map(
        local,
        mesh=mesh,
        in_specs=(P("mode", "col", None), P()),
        out_specs=(P(None, "col", "mode"), P(), P()),
        check_vma=False,
    )
```

```python
import functools

import jax
import jax.numpy as jnp
from jax import lax
from jax.experimental import pallas as pl
from jax.experimental.pallas import tpu as pltpu
from jax.sharding import PartitionSpec as P

MESH = pl.DeviceIdType.MESH
ITERS = 3
R = 512
NX, NY, NZ = 4, 8, 8
PLANE = 2 * NX * NY
STARTS = (0, 512, 896, 1152)
N = 128
precise = lax.Precision.HIGHEST


def dot_nt(a, b):
    return lax.dot_general(a, b, (((1,), (1,)), ((), ())), preferred_element_type=jnp.float32)


def gather_kernel(t_ref, unf_ref, g_ref, hi, lo, gp, rc, rx, a2, rz, a3, ry, full,
                  own_sem, s_a2a, r_a2a, s_c, r_c, s_x, r_x, s_z, r_z, s_y, r_y,
                  s_fz, s_fx, s_fc, r_fc, r_full):
    m, z = lax.axis_index("mode"), lax.axis_index("col")
    c = lax.rem(m, 2)
    x = lax.rem(m // 2, NX)
    y = m // (2 * NX)

    def index(yy, xx, cc):
        return (yy * NX + xx) * 2 + cc

    def remote(src, dst, send_sem, recv_sem, mode, col):
        return pltpu.make_async_remote_copy(
            src, dst, send_sem, recv_sem, device_id={"mode": mode, "col": col}, device_id_type=MESH)

    def near(dy, dx, dc):
        return index(lax.rem(y + dy, NY), lax.rem(x + dx, NX), lax.rem(c + dc, 2))

    barrier = pltpu.get_barrier_semaphore()

    def greet(mode, col):
        pl.semaphore_signal(barrier, inc=1, device_id={"mode": mode, "col": col}, device_id_type=MESH)

    def greet_far(k, carry):
        for dy in (4, 3, 5, 2, 6, 1, 7, 0):
            greet(near(dy, k // 2, lax.rem(k, 2)), z)
        return carry

    for k in (4, 3, 5, 2, 6, 1, 7):
        greet(m, lax.rem(z + k, NZ))
    lax.fori_loop(1, 2 * NX, greet_far, 0)
    for dy in (4, 3, 5, 2, 6, 1, 7):
        greet(near(dy, 0, 0), z)
    pl.semaphore_wait(barrier, PLANE - 1 + NZ - 1)

    def columns(d, s):
        return t_ref.at[:, s, pl.ds(pl.multiple_of(d * 256, 256), 256)]

    def slab(src, s):
        return unf_ref.at[src, :, pl.ds(s * 256, 256)]

    def straight(d, src, s):
        return remote(columns(d, s), slab(src, s), s_a2a.at[s, d], r_a2a.at[s, src], d, z)

    def send(k, carry):
        for dy in (4, 1, 7, 2, 6, 3, 5, 0):
            for s in range(2):
                straight(near(dy, k // 2, lax.rem(k, 2)), m, s).start()
        return carry

    for dy in (4, 1, 7, 2, 6, 3, 5):
        for s in range(2):
            straight(near(dy, 0, 0), m, s).start()
    lax.fori_loop(1, 2 * NX, send, 0)
    own = [pltpu.make_async_copy(columns(m, s), slab(m, s), own_sem.at[s]) for s in range(2)]
    for copy in own:
        copy.start()
    for copy in own:
        copy.wait()

    def arrived(k, carry):
        d = lax.rem(m + k, PLANE)
        for s in range(2):
            straight(d, d, s).wait()
        return carry

    lax.fori_loop(1, PLANE, arrived, 0)

    unfold = unf_ref[...].reshape(R, 512)
    high = unfold.astype(jnp.bfloat16)
    hi[...] = high
    lo[...] = (unfold - high.astype(jnp.float32)).astype(jnp.bfloat16)
    scale = 1.0 / (512 * PLANE * NZ)
    gp[...] = jnp.zeros_like(gp)
    for i in range(4):
        h = hi[pl.ds(i * N, N), :]
        l = lo[pl.ds(i * N, N), :]
        rest = pl.ds(i * N, R - i * N)
        part = (dot_nt(h, hi[rest, :]) + (dot_nt(h, lo[rest, :]) + dot_nt(l, hi[rest, :]))) * scale
        for j in range(4 - i):
            tile = part[:, j * N:(j + 1) * N].reshape(8, 2, 8, N)
            q, lane = divmod(STARTS[i] // N + j, 3)
            for rg in range(2):
                gp[:, rg * 4 + q, :, lane * N:(lane + 1) * N] = tile[:, rg]

    def c_copy(to):
        return remote(gp.at[(1 - c) * NX + to], rc.at[to], s_c.at[to], r_c.at[to], index(y, x, 1 - c), z)

    ring_x = [lax.rem(x + k, NX) for k in (2, 1, 3, 0)]
    ring_z = [lax.rem(z + k, NZ) for k in (4, 3, 5, 2, 6, 1, 7)]
    for to in ring_x:
        c_copy(to).start()
    for to in ring_x:
        c_copy(to).wait()
        rc[to] += gp[c * NX + to]

    def fitting(piece, act):
        for last in (False, True):
            width = N if last else 3 * N

            @pl.when((lax.rem(piece, 4) == 3) == last)
            def _():
                act(pl.ds(0, width))

    def x_copy(to, piece, src, lanes):
        return remote(rc.at[to, piece, :, lanes], rx.at[src, piece, :, lanes], s_x.at[to, piece], r_x.at[src, piece], index(y, to, c), z)

    def z_copy(to, src):
        return remote(a2.at[to], rz.at[src], s_z.at[to], r_z.at[src], m, to)

    for piece in ring_z + [z]:
        fitting(piece, lambda lanes: [x_copy(to, piece, x, lanes).start() for to in ring_x[:3]])
    rx[x] = rc[x]
    for piece in ring_z + [z]:
        fitting(piece, lambda lanes: [x_copy(to, piece, to, lanes).wait_recv() for to in ring_x[:3]])
        a2[piece] = (rx[0, piece] + rx[1, piece]) + (rx[2, piece] + rx[3, piece])
        if piece is not z:
            z_copy(piece, z).start()
    rz[z] = a2[z]
    for to in reversed(ring_z):
        z_copy(to, to).wait()
    a3[...] = ((rz[0] + rz[1]) + (rz[2] + rz[3])) + ((rz[4] + rz[5]) + (rz[6] + rz[7]))

    def y_copy(to, src):
        return remote(a3, ry.at[src], s_y.at[to], r_y.at[src], index(to, x, c), z)

    ring_y = [lax.rem(y + k, NY) for k in (4, 3, 5, 2, 6, 1, 7)]
    for to in ring_y:
        y_copy(to, y).start()
    ry[y] = a3[...]
    for to in reversed(ring_y):
        y_copy(to, to).wait()
    full[c, x, z] = ((ry[0] + ry[1]) + (ry[2] + ry[3])) + ((ry[4] + ry[5]) + (ry[6] + ry[7]))

    def fz_copy(to, src):
        return remote(full.at[c, x, src], full.at[c, x, src], s_fz.at[to], r_full.at[c, x, src], m, to)

    def fx_copy(to, src, piece, lanes):
        part = full.at[c, src, piece, :, lanes]
        return remote(part, part, s_fx.at[to, piece], r_full.at[c, src, piece], index(y, to, c), z)

    def fc_copy(cc, piece):
        return remote(full.at[cc, :, piece], full.at[cc, :, piece], s_fc.at[piece], r_fc.at[piece], index(y, x, 1 - c), z)

    def pass_on(piece):
        fitting(piece, lambda lanes: [fx_copy(to, x, piece, lanes).start() for to in ring_x[:3]])

    for to in ring_z:
        fz_copy(to, z).start()
    pass_on(z)
    for src in reversed(ring_z):
        fz_copy(src, src).wait_recv()
        pass_on(src)
    for piece in [z] + ring_z[::-1]:
        fitting(piece, lambda lanes: [fx_copy(src, src, piece, lanes).wait_recv() for src in ring_x[:3]])
        fc_copy(c, piece).start()
    for piece in [z] + ring_z[::-1]:
        fc_copy(1 - c, piece).wait_recv()

    whole = full[...].reshape(16, 4, 8, 384)
    for i in range(4):
        for j in range(i, 4):
            q, lane = divmod(STARTS[i] // N + j - i, 3)
            block = whole[:, q, :, lane * N:(lane + 1) * N].reshape(N, N)
            g_ref[pl.ds(i * N, N), pl.ds(j * N, N)] = block
            if i != j:
                g_ref[pl.ds(j * N, N), pl.ds(i * N, N)] = block.T

    def sent_x(k, carry):
        fitting(k, lambda lanes: [copy.wait_send() for to in ring_x[:3] for copy in (x_copy(to, k, x, lanes), fx_copy(to, x, k, lanes))])
        fc_copy(c, k).wait_send()
        return carry

    lax.fori_loop(0, NZ, sent_x, 0)
    for to in ring_z:
        fz_copy(to, z).wait_send()


def gathered(tensor):
    f32 = jnp.float32
    dma = pltpu.SemaphoreType.DMA
    vmem = pl.BlockSpec(memory_space=pltpu.VMEM)
    piece = (8, 384)
    return pl.pallas_call(
        gather_kernel,
        out_shape=(jax.ShapeDtypeStruct((PLANE, 8, 512), f32), jax.ShapeDtypeStruct((R, R), f32)),
        in_specs=[pl.BlockSpec(memory_space=pltpu.HBM)],
        out_specs=(vmem, vmem),
        scratch_shapes=[
            pltpu.VMEM((R, 512), jnp.bfloat16),
            pltpu.VMEM((R, 512), jnp.bfloat16),
            pltpu.VMEM((2 * NX, NZ, *piece), f32),
            pltpu.VMEM((NX, NZ, *piece), f32),
            pltpu.VMEM((NX, NZ, *piece), f32),
            pltpu.VMEM((NZ, *piece), f32),
            pltpu.VMEM((NZ, *piece), f32),
            pltpu.VMEM(piece, f32),
            pltpu.VMEM((NY, *piece), f32),
            pltpu.VMEM((2, NX, NZ, *piece), f32),
            dma((2,)), dma((2, PLANE)), dma((2, PLANE)),
            dma((NX,)), dma((NX,)), dma((NX, NZ)), dma((NX, NZ)), dma((NZ,)), dma((NZ,)), dma((NY,)), dma((NY,)),
            dma((NZ,)), dma((NX, NZ)), dma((NZ,)), dma((NZ,)), dma((2, NX, NZ)),
        ],
        compiler_params=pltpu.CompilerParams(
            collective_id=0, has_side_effects=True, vmem_limit_bytes=40 * 2**20),
    )(pltpu.with_memory_space_constraint(tensor, pltpu.HBM))


def dot_tn(a, b):
    return lax.dot_general(a, b, (((0,), (0,)), ((), ())), preferred_element_type=jnp.float32)


def dot_full(a, b, da, db):
    return lax.dot_general(
        a, b, (((da,), (db,)), ((), ())), precision=precise, preferred_element_type=jnp.float32)


def row_of(tile, j):
    return jnp.broadcast_to(tile[j:j + 1, :], (8, N))


def column_of(tile, j):
    return jnp.broadcast_to(tile[:, j:j + 1], (8, N))


def split(a):
    high = a.astype(jnp.bfloat16)
    return high, (a - high.astype(jnp.float32)).astype(jnp.bfloat16)


def dot_split(a, b, da, db):
    (a_high, a_low), (b_high, b_low) = split(a), split(b)

    def dot(p, q):
        return lax.dot_general(p, q, (((da,), (db,)), ((), ())), preferred_element_type=jnp.float32)

    return dot(a_high, b_high) + (dot(a_high, b_low) + dot(a_low, b_high))


def factor(m_ref, u_ref, v_ref):
    line, lane = (lax.broadcasted_iota(jnp.int32, (8, N), d) for d in range(2))
    for first in range(0, N, 32):
        last = first + 32
        m = [m_ref[first + 8 * i:first + 8 * i + 8, :] for i in range(4)]
        for b in range(4):
            start = first + 8 * b
            stop = start + 8
            inside = (lane >= start) & (lane < stop)
            columns = {i: [column_of(m[i], start + k) for k in range(8)] for i in range(b, 4)}
            for i in range(b, 4):
                m[i] = jnp.where(inside, (lane - start == line).astype(jnp.float32) if i == b else 0.0, m[i])
            pivots = jnp.zeros((8, N), jnp.float32)
            for j in range(0, 8, 2):
                row_columns = {k: row_of(columns[b][k], j) for k in range(j, 8)}
                pivot, beside = row_columns[j], row_columns[j + 1]
                square = pivot * row_of(columns[b][j + 1], j + 1) - beside * beside
                inverse, later = 1.0 / pivot, pivot * (1.0 / square)
                pivots = jnp.where(line == j, pivot, pivots)
                row = row_of(m[b], j)
                for i in range(b, 4):
                    ratio = columns[i][j] * inverse
                    if i == b:
                        ratio = jnp.where(line > j, ratio, 0.0)
                    m[i] = m[i] - ratio * row
                    for k in range(j + 1, 8):
                        columns[i][k] = columns[i][k] - ratio * row_columns[k]
                row_columns = {k: row_of(columns[b][k], j + 1) for k in range(j + 1, 8)}
                pivots = jnp.where(line == j + 1, row_columns[j + 1], pivots)
                row = row_of(m[b], j + 1)
                for i in range(b, 4):
                    ratio = columns[i][j + 1] * later
                    if i == b:
                        ratio = jnp.where(line > j + 1, ratio, 0.0)
                    m[i] = m[i] - ratio * row
                    for k in range(j + 2, 8):
                        columns[i][k] = columns[i][k] - ratio * row_columns[k]
            root = lax.rsqrt(pivots)
            root = root * (1.5 - 0.5 * (pivots * root) * root)
            m[b] = m[b] * root
            corner = jnp.zeros((8, N), jnp.float32)
            for k in range(8):
                corner = jnp.where((lane == start + k) & (line <= k), columns[b][k], corner)
            u_ref[start:stop, :] = jnp.where(lane >= stop, m[b], corner * root)
            v_ref[start:stop, :] = jnp.where(lane < stop, m[b], 0.0)
        if last < N:
            done = jnp.concatenate(m, axis=0)
            left = done.T[last:, :]
            right = jnp.concatenate(
                [jnp.where((lane >= first + 8 * b + 8) & (lane < last), 0.0, m[b]) for b in range(4)], axis=0)
            update = dot_full(left, right, 1, 0)
            wide = lax.broadcasted_iota(jnp.int32, (N - last, N), 1)
            m_ref[last:, :] = jnp.where((wide >= first) & (wide < last), 0.0, m_ref[last:, :]) - update


def factor_kernel(g_ref, initial_ref, basis_ref, triangle_ref, rest_ref, high_ref, low_ref, m_ref, u_ref, v_ref):
    c = lax.rem(lax.axis_index("mode"), 2)

    @pl.when(c == 0)
    def _():
        for k in range(4):
            own, after = pl.ds(k * N, N), pl.ds((k + 1) * N, R - (k + 1) * N)
            left_ref = rest_ref if k else g_ref
            m_ref[...] = left_ref[own, own]
            if k:
                triangle_ref[own, pl.ds(0, k * N)] = jnp.zeros((N, k * N), jnp.float32)
            factor(m_ref, u_ref, v_ref)
            triangle_ref[own, own] = u_ref[...]
            if k < 3:
                panel = dot_split(v_ref[...], left_ref[own, after], 1, 0)
                triangle_ref[own, after] = panel
                parts = split(panel)
                for i in range(k + 1, 4):
                    own_part = [part[:, (i - k - 1) * N:(i - k) * N] for part in parts]
                    high, low = [part[:, (i - k - 1) * N:] for part in parts]
                    there = pl.ds(i * N, N), pl.ds(i * N, R - i * N)
                    rest_ref[there] = left_ref[there] - (
                        dot_tn(own_part[0], high) + (dot_tn(own_part[0], low) + dot_tn(own_part[1], high)))

    @pl.when(c == 1)
    def _():
        high_ref[...], low_ref[...] = split(g_ref[...])
        basis_ref[...] = initial_ref[...]

        def sweep(step, carry):
            high, low = split(basis_ref[...])
            both = jnp.dot(high_ref[...], jnp.concatenate([high, low], axis=1), preferred_element_type=jnp.float32)
            product = both[:, :N] + (both[:, N:] + jnp.dot(low_ref[...], high, preferred_element_type=jnp.float32))
            basis_ref[...] = product
            m_ref[...] = dot_full(product, product, 0, 0)
            factor(m_ref, u_ref, v_ref)
            basis_ref[...] = dot_split(basis_ref[...], v_ref[...], 1, 1)
            return carry

        lax.fori_loop(0, ITERS, sweep, 0)


def factored(gram, initial):
    f32 = jnp.float32
    vmem = pl.BlockSpec(memory_space=pltpu.VMEM)
    square = pltpu.VMEM((N, N), f32)
    return pl.pallas_call(
        factor_kernel,
        out_shape=(jax.ShapeDtypeStruct((R, N), f32), jax.ShapeDtypeStruct((R, R), f32)),
        in_specs=[vmem, vmem],
        out_specs=(vmem, vmem),
        scratch_shapes=[
            pltpu.VMEM((R, R), f32), pltpu.VMEM((R, R), jnp.bfloat16), pltpu.VMEM((R, R), jnp.bfloat16), square, square, square],
        compiler_params=pltpu.CompilerParams(vmem_limit_bytes=16 * 2**20),
    )(gram, initial)


def exchange_kernel(basis_ref, triangle_ref, basis_out, triangle_out, send_sem, recv_sem):
    m, z = lax.axis_index("mode"), lax.axis_index("col")
    c = lax.rem(m, 2)
    partner = {"mode": m + 1 - 2 * c, "col": z}
    barrier = pltpu.get_barrier_semaphore()
    pl.semaphore_signal(barrier, inc=1, device_id=partner, device_id_type=MESH)
    pl.semaphore_wait(barrier, 1)

    def over(src, dst, k):
        return pltpu.make_async_remote_copy(
            src, dst, send_sem.at[k], recv_sem.at[k], device_id=partner, device_id_type=MESH)

    def upper(ref, k):
        return ref.at[pl.ds(k * N, N), pl.ds(k * N, R - k * N)]

    strips = [over(upper(triangle_ref, k), upper(triangle_out, k), k) for k in range(4)]
    whole = over(basis_ref, basis_out, 4)

    @pl.when(c == 0)
    def _():
        for strip in strips:
            strip.start()
        triangle_out[...] = triangle_ref[...]
        whole.wait_recv()
        for strip in strips:
            strip.wait_send()

    @pl.when(c == 1)
    def _():
        whole.start()
        basis_out[...] = basis_ref[...]
        for k in range(1, 4):
            triangle_out[pl.ds(k * N, N), pl.ds(0, k * N)] = jnp.zeros((N, k * N), jnp.float32)
        for strip in strips:
            strip.wait_recv()
        whole.wait_send()


def exchanged(basis, triangle):
    dma = pltpu.SemaphoreType.DMA
    vmem = pl.BlockSpec(memory_space=pltpu.VMEM)
    return pl.pallas_call(
        exchange_kernel,
        out_shape=tuple(jax.ShapeDtypeStruct(a.shape, a.dtype) for a in (basis, triangle)),
        in_specs=[vmem, vmem],
        out_specs=(vmem, vmem),
        scratch_shapes=[dma((5,)), dma((5,))],
        compiler_params=pltpu.CompilerParams(
            collective_id=1, has_side_effects=True, vmem_limit_bytes=8 * 2**20),
    )(basis, triangle)


def core_kernel(basis_ref, triangle_ref, blocks_ref, core_out, basis_out, triangle_out, core_ref, sem):
    copies = [
        pltpu.make_async_copy(triangle_ref, triangle_out, sem.at[0]),
        pltpu.make_async_copy(basis_ref, basis_out, sem.at[1]),
    ]
    for copy in copies:
        copy.start()
    unfold = blocks_ref[...].reshape(R, 512)
    core = dot_split(basis_ref[...], unfold, 0, 0)
    for part in range(2):
        rows = pl.ds(part * 64, 64)
        for s in range(2):
            core_ref[rows, s, :] = core[part * 64:(part + 1) * 64, s * 256:(s + 1) * 256]
        copies.append(pltpu.make_async_copy(core_ref.at[rows], core_out.at[rows], sem.at[2 + part]))
        copies[-1].start()
    for copy in copies:
        copy.wait()


def projected(basis, triangle, blocks):
    vmem, anywhere = (pl.BlockSpec(memory_space=space) for space in (pltpu.VMEM, pl.ANY))
    return pl.pallas_call(
        core_kernel,
        out_shape=tuple(jax.ShapeDtypeStruct(shape, jnp.float32) for shape in ((N, 2, 256), (R, N), (R, R))),
        in_specs=[vmem] * 3,
        out_specs=(anywhere, anywhere, anywhere),
        scratch_shapes=[pltpu.VMEM((N, 2, 256), jnp.float32), pltpu.SemaphoreType.DMA((4,))],
        compiler_params=pltpu.CompilerParams(vmem_limit_bytes=16 * 2**20),
    )(basis, triangle, blocks)


def local(tensor, initial):
    blocks, gram = gathered(tensor)
    basis, triangle = exchanged(*factored(gram, initial))
    return projected(basis, triangle, blocks)


def solution(mesh):
    return jax.shard_map(
        local,
        mesh=mesh,
        in_specs=(P("mode", "col", None), P()),
        out_specs=(P(None, "col", "mode"), P(), P()),
        check_vma=False,
    )
```
